128 devices in a mesh: replica: 8 (over y, z_hi), shard: 16 (over z_lo, x, core).
Axes of the slice: x: 4, y: 4, z: 4 (z_hi: 2, z_lo: 2; z = z_hi * 2 + z_lo), core: 2. Of those that a mesh axis runs over, the one named last changes fastest.
Arguments:
- images: float32 [384, 7, 7, 1024], P(('replica', 'shard')), may hold values from -6 to 6
- filters: float32 [1, 1024, 9216], P(None, 'shard'), may hold values from -0.0625 to 0.0625
- out_grad: float32 [384, 7, 7, 1024], P(('replica', 'shard')), may hold values from -6 to 6
Outputs:
- conv_out: float32 [384, 7, 7, 1024], P(('replica', 'shard'))
- filter_grad: float32 [1, 1024, 9216], P(None, 'shard', 'replica')
The draws below stay inside these ranges and needn't reach their ends.
All inputs are finite; a program needn't handle non-finite values.
Results may differ from the reference program's by a relative error of at most 0.0003.
Values sent between devices are 32-bit elements; how exact they have to be, the bound alone decides.
A program may use at most 256 MiB of HBM per device.

```python
import jax
import jax.numpy as jnp
from jax import lax

GROUPS = 1
H = 7
W = 7
GW = 1024
CH = 1024
BATCH = 384


def block_levels(own_key, extent, cuts, smallest, largest):
    loudness, own = 1.0, jax.random.fold_in(own_key, 6)
    for position, shards_of in cuts:
        steps = jnp.exp(jax.random.uniform(jax.random.fold_in(own, position), (shards_of,), jnp.float32, smallest / len(cuts), largest / len(cuts)))
        loudness = loudness * jnp.repeat(steps, extent[position] // shards_of).reshape([-1 if axis == position else 1 for axis in range(len(extent))])
    return loudness


def centred(key, dims, deviation, bound, pieces=(), held_as=jnp.bfloat16):
    result = jax.random.normal(key, dims, jnp.float32) * deviation
    if len(pieces) > 0:
        result = block_levels(key, dims, pieces, -0.22, 0.18) * result
    return jnp.clip(result, min=-bound, max=bound).astype(held_as)


def setup_inputs(seed: int = 0) -> dict:
    key_list = jax.random.split(jax.random.key(seed), 4)
    return {
        "images": centred(key_list[0], (BATCH, H, W, CH), 1.0, 6.0, ((0, 128),), jnp.float32),
        "filters": centred(key_list[1], (GROUPS, GW, 9 * GW), (9 * GW) ** -0.5, 0.0625, ((1, 16),), jnp.float32),
        "out_grad": centred(key_list[2], (BATCH, H, W, CH), 1.0, 6.0, ((0, 128),), jnp.float32),
    }


def conv_patches(block):
    batch, rows, cols, chans = block.shape
    padded = jnp.pad(block, ((0, 0), (1, 1), (1, 1), (0, 0)))
    taps = [padded[:, a:a + rows, c:c + cols, :] for a in range(3) for c in range(3)]
    return jnp.concatenate(taps, axis=3).reshape(batch * rows * cols, 9 * chans)


def reference(images, filters, out_grad):
    batch, rows, cols, chans = images.shape
    width = filters.shape[1]
    count = filters.shape[0]

    def one_group(group):
        start = (group * width).astype(jnp.int32)
        patch = conv_patches(lax.dynamic_slice_in_dim(images, start, width, 3))
        grad_rows = lax.dynamic_slice_in_dim(out_grad, start, width, 3).reshape(-1, width)
        weight = lax.dynamic_index_in_dim(filters, group, 0, keepdims=False)
        output = lax.dot_general(patch, weight, (((1,), (1,)), ((), ())), precision=lax.Precision.HIGHEST, preferred_element_type=jnp.float32)
        grads = lax.dot_general(grad_rows, patch, (((0,), (0,)), ((), ())), precision=lax.Precision.HIGHEST, preferred_element_type=jnp.float32)
        return output, grads

    outputs, grads = lax.map(one_group, jnp.arange(count, dtype=jnp.int32))
    conv_out = jnp.transpose(outputs, (1, 0, 2)).reshape(batch, rows, cols, chans)
    return conv_out, grads
```

```python
import functools

import jax
import jax.numpy as jnp
from jax import lax
from jax.experimental import pallas as pl
from jax.experimental.pallas import tpu as pltpu
from jax.sharding import PartitionSpec as P

MESH = pl.DeviceIdType.MESH
F32 = jnp.float32
BF16 = jnp.bfloat16
NX = 4
NY = 4
NCH = 4
CW = 256
ROWS = 147
WIRE = 152
SLOT = 160
CUT = 80
NSLOT = 16
TOTAL = SLOT * NSLOT
GROUP = 4 * SLOT
OWN = 64
DELTA = [7 * (t // 3 - 1) + (t % 3 - 1) for t in range(9)]

S_OWN, S_A, S_B, S_C, S_D, S_E, S_F, S_G = 0, 2, 4, 6, 8, 10, 12, 14
K_A, K_B, K_C, K_D1, K_D2, K_E, K_F, K_G1, K_G2, K_P = range(10)
NK = K_P + 8
INVERSE = [0, 2, 1, 3, 4, 6, 5, 7]


def kernel(
    x_ref, f_ref, g_ref, out_ref, fg_ref,
    xg, x3, f3t, f8t, gall, gsh, gsl, maskc, maskg, yacc, fgu, r1, r2, sy, fin, zs, zr, cs, cp, cf,
    xsend, xrecv, gsend, grecv, csend, crecv, rsend, rrecv, zsem,
):
    rep = lax.axis_index("replica")
    shard = lax.axis_index("shard")
    core = lax.rem(shard, 2)
    x = lax.rem(lax.div(shard, 2), NX)
    z = lax.div(shard, 2 * NX)
    y = lax.div(rep, 2)
    zh = lax.rem(rep, 2)

    def at(dx, dz, dc=0):
        xx = lax.rem(x + dx + NX, NX)
        zz = lax.rem(z + dz, 2)
        cc = lax.rem(core + dc, 2)
        return (rep, zz * 2 * NX + xx * 2 + cc)

    def chip_of(dx, dz):
        return lax.rem(z + dz, 2) * NX + lax.rem(x + dx + NX, NX)

    rel = [(0, 0), (-1, 0), (1, 0), (0, 1), (2, 0), (-1, 1), (1, 1), (2, 1)]
    partner = at(0, 0, 1)
    yp = lax.rem(y + 1, NY)
    ym = lax.rem(y + NY - 1, NY)
    y2 = lax.rem(y + 2, NY)
    up = (yp * 2 + zh, shard)
    down = (ym * 2 + zh, shard)
    far = (y * 2 + 1 - zh, shard)

    peers = [at(*rel[k]) for k in range(1, 8)] + [partner, up, down, far]
    barrier = pltpu.get_barrier_semaphore()
    for peer in peers:
        pl.semaphore_signal(barrier, inc=1, device_id=peer, device_id_type=MESH)
    pl.semaphore_wait(barrier, len(peers))

    def remote(src, dst, ssem, rsem, dev):
        return pltpu.make_async_remote_copy(
            src_ref=src, dst_ref=dst, send_sem=ssem, recv_sem=rsem, device_id=dev, device_id_type=MESH
        )

    def grad_copy(k):
        if k == 0:
            return None
        cols = pl.ds(pl.multiple_of(128 * chip_of(*rel[k]), 128), 128)
        return remote(g_ref.at[:, cols], gall.at[2 * INVERSE[k]], gsend.at[k], grecv.at[INVERSE[k]], at(*rel[k]))

    def grad_in(k):
        return remote(gall.at[2 * k], gall.at[2 * k], gsend.at[k], grecv.at[k], at(*rel[k]))

    def grad_pass(k):
        if k == 0:
            cols = pl.ds(pl.multiple_of(128 * chip_of(0, 0), 128), 128)
            src = g_ref.at[:, cols]
        else:
            src = gall.at[2 * k]
        return remote(src, gall.at[2 * k + 1], gsend.at[8 + k], grecv.at[8 + k], partner)

    def own(j):
        return x_ref.at[:, pl.ds(pl.multiple_of(CW * j, CW), CW)]

    def x_copy(j, kind):
        lo, hi = pl.ds(0, CUT), pl.ds(CUT, WIRE - CUT)
        if kind >= K_P:
            k = kind - K_P
            src = own(j) if k == 0 else xg.at[j, 2 * k]
            dst, dev = xg.at[j, 2 * k + 1], partner
        elif kind == K_A:
            src, dst, dev = own(j), xg.at[j, S_A], at(1, 0)
        elif kind == K_B:
            src, dst, dev = own(j), xg.at[j, S_B], at(-1, 0)
        elif kind == K_C:
            src, dst, dev = own(j), xg.at[j, S_C], at(0, 1)
        elif kind == K_D1:
            src, dst, dev = xg.at[j, S_A, lo], xg.at[j, S_D, lo], at(1, 0)
        elif kind == K_D2:
            src, dst, dev = xg.at[j, S_B, hi], xg.at[j, S_D, hi], at(-1, 0)
        elif kind == K_E:
            src, dst, dev = xg.at[j, S_C], xg.at[j, S_E], at(1, 0)
        elif kind == K_F:
            src, dst, dev = xg.at[j, S_C], xg.at[j, S_F], at(-1, 0)
        elif kind == K_G1:
            src, dst, dev = xg.at[j, S_D, lo], xg.at[j, S_G, lo], at(0, 1)
        else:
            src, dst, dev = xg.at[j, S_D, hi], xg.at[j, S_G, hi], at(0, 1)
        return remote(src, dst, xsend.at[j, kind], xrecv.at[j, kind], dev)

    def x_own(j):
        for kind in (K_A, K_B, K_C, K_P):
            x_copy(j, kind).start()

    for k in (4, 7, 1, 2, 5, 6, 3):
        grad_copy(k).start()
    grad_pass(0).start()
    x_own(0)
    x_own(1)

    for j in range(NCH):
        xg[j, 0] = x_ref[:, CW * j : CW * (j + 1)]
    gall[0] = g_ref[:, pl.ds(pl.multiple_of(128 * chip_of(0, 0), 128), 128)]

    lane = lax.broadcasted_iota(jnp.int32, (SLOT, 128), 1)
    low = lane < OWN
    pos = lax.broadcasted_iota(jnp.int32, (SLOT, 128), 0).astype(F32)
    rem = pos - 49.0 * jnp.floor((pos + 0.5) * (1.0 / 49.0))
    hh = jnp.floor((rem + 0.5) * (1.0 / 7.0))
    ww = rem - 7.0 * hh
    for pair in range(5):
        t0, t1 = 2 * pair, min(2 * pair + 1, 8)
        da = jnp.where(low, float(t0 // 3 - 1), float(t1 // 3 - 1))
        dc = jnp.where(low, float(t0 % 3 - 1), float(t1 % 3 - 1))
        for sign, mask in ((1.0, maskc), (-1.0, maskg)):
            h1, w1 = hh + sign * da, ww + sign * dc
            inside = jnp.minimum(jnp.minimum(h1, 6.0 - h1), jnp.minimum(w1, 6.0 - w1)) > -0.5
            mask[pair] = jnp.where(inside, 1.0, 0.0)

    def halves(v):
        hi = v.astype(BF16)
        lo = (v - hi.astype(F32)).astype(BF16)
        return hi, lo

    @pl.loop(0, NCH)
    def _(j):
        for pair in range(4):
            parts = []
            for t in (2 * pair, 2 * pair + 1):
                parts.append(f_ref[:, pl.ds(pl.multiple_of(t * 1024 + CW * j, CW), CW)])
            hi, lo = halves(jnp.concatenate(parts, axis=0).T)
            cols = slice(128 * pair, 128 * pair + 128)
            f3t[j, 0:CW, cols] = hi
            f3t[j, CW : 2 * CW, cols] = hi
            f3t[j, 2 * CW : 3 * CW, cols] = lo
        f8 = f_ref[:, pl.ds(pl.multiple_of(8 * 1024 + CW * j, CW), CW)]
        hi8 = f8.astype(BF16).astype(F32)
        both = jnp.concatenate([hi8, f8 - hi8], axis=0).T.astype(BF16)
        f8t[j, 0:CW, :] = both
        f8t[j, CW : 2 * CW, :] = both

    for k in (1, 2, 3, 4, 5, 6, 7):
        grad_in(k).wait_recv()
        grad_pass(k).start()
    for k in range(8):
        grad_pass(k).wait_recv()

    lane4 = lax.broadcasted_iota(jnp.int32, (GROUP, 128), 1)
    low4 = lane4 < OWN
    mine4 = (lane4 < OWN) == (core == 0)

    def padded(v):
        return jnp.concatenate([v, jnp.zeros((SLOT - WIRE, v.shape[1]), v.dtype)], axis=0)

    @pl.loop(0, 4)
    def _(m):
        g = jnp.concatenate([padded(gall[4 * m + i]) for i in range(4)], axis=0)
        gg = jnp.where(mine4, g, pltpu.roll(g, OWN, 1))
        cols = pl.ds(pl.multiple_of(GROUP * m, GROUP), GROUP)
        for pair in range(5):
            t0, t1 = 2 * pair, min(2 * pair + 1, 8)
            first = pltpu.roll(gg, DELTA[t0] % GROUP, 0)
            second = first if t1 == t0 else pltpu.roll(gg, DELTA[t1] % GROUP, 0)
            mask = jnp.concatenate([maskg[pair]] * 4, axis=0)
            hi, lo = halves((jnp.where(low4, first, second) * mask).T)
            gsh[128 * pair : 128 * pair + 128, cols] = hi
            gsl[128 * pair : 128 * pair + 128, cols] = lo

    def window(yy, j):
        return pl.ds(lax.div(9 * yy - j + 3, 4), 3)

    def r_copy(j, kind):
        if kind == 0:
            src, dst, dev = fgu.at[j, 0, window(y2, j)], r1.at[j, 0], up
        elif kind == 1:
            src, dst, dev = fgu.at[j, 1, window(y2, j)], r1.at[j, 1], down
        elif kind == 2:
            src, dst, dev = fgu.at[j, 1, window(yp, j)], r2.at[j, 1], up
        elif kind == 3:
            src, dst, dev = fgu.at[j, 0, window(ym, j)], r2.at[j, 2], down
        elif kind == 4:
            src, dst, dev = sy.at[j, 0], r2.at[j, 0], up
        else:
            src, dst, dev = sy.at[j, 1], r2.at[j, 3], down
        return remote(src, dst, rsend.at[j, kind], rrecv.at[j, kind], dev)

    def rs_mid(j):
        r_copy(j, 0).wait_recv()
        sy[j, 0] = fgu[j, 0, window(yp, j)] + r1[j, 0]
        r_copy(j, 4).start()
        r_copy(j, 1).wait_recv()
        sy[j, 1] = fgu[j, 1, window(ym, j)] + r1[j, 1]
        r_copy(j, 5).start()

    def rs_end(j):
        for kind in (2, 3, 4, 5):
            r_copy(j, kind).wait_recv()
        fin[j, 0] = fgu[j, 0, window(y, j)] + r2[j, 0] + r2[j, 2]
        fin[j, 1] = fgu[j, 1, window(y, j)] + r2[j, 1] + r2[j, 3]

    def nn(a, b):
        return lax.dot_general(a, b, (((1,), (0,)), ((), ())), preferred_element_type=F32)

    def conv(j, first, count):
        @pl.loop(first, first + count)
        def _(m):
            rows = pl.ds(pl.multiple_of(GROUP * m, GROUP), GROUP)
            main = nn(x3[j, rows, :], f3t[j])
            last = nn(x3[j, rows, 0 : 2 * CW], f8t[j])

            @pl.when(j == 0)
            def _():
                yacc[rows, 0:512] = main
                yacc[rows, 512:640] = last

            @pl.when(j > 0)
            def _():
                yacc[rows, 0:512] += main
                yacc[rows, 512:640] += last

    def to_partner(j, *slots):
        for s in slots:
            x_copy(j, K_P + s // 2).start()

    def chunk(j, carry):
        for kind in (K_A, K_B, K_C):
            x_copy(j, kind).wait_recv()
        for kind in (K_D1, K_D2, K_E, K_F):
            x_copy(j, kind).start()
        to_partner(j, S_A, S_B, S_C)

        @pl.when(j < NCH - 2)
        def _():
            x_own(j + 2)

        @pl.when(j > 0)
        def _():
            conv(j - 1, 0, 2)

        x_copy(j, K_D1).wait_recv()
        x_copy(j, K_G1).start()
        x_copy(j, K_D2).wait_recv()
        x_copy(j, K_G2).start()
        x_copy(j, K_E).wait_recv()
        x_copy(j, K_F).wait_recv()
        to_partner(j, S_D, S_E, S_F)

        @pl.when(j > 0)
        def _():
            rs_mid(j - 1)
            conv(j - 1, 2, 2)
            rs_end(j - 1)

        x_copy(j, K_G1).wait_recv()
        x_copy(j, K_G2).wait_recv()
        to_partner(j, S_G)
        for k in range(8):
            x_copy(j, K_P + k).wait_recv()

        @pl.loop(0, NSLOT)
        def _(s):
            hi, lo = halves(padded(xg[j, s]))
            rows = pl.ds(pl.multiple_of(SLOT * s, SLOT), SLOT)
            x3[j, rows, 0:CW] = hi
            x3[j, rows, CW : 2 * CW] = lo
            x3[j, rows, 2 * CW : 3 * CW] = hi

        res = nn(gsh[0:576, :], x3[j, :, 0:CW])
        res += nn(gsl[0:576, :], x3[j, :, 0:CW])
        res += nn(gsh[0:576, :], x3[j, :, CW : 2 * CW])
        for h in range(2):
            for t in range(9):
                fgu[j, h, t] = res[OWN * t : OWN * (t + 1), 128 * h : 128 * (h + 1)]
            fgu[j, h, 9] = jnp.zeros((OWN, 128), F32)
        for kind in (0, 1, 2, 3):
            r_copy(j, kind).start()
        return carry

    lax.fori_loop(0, NCH, chunk, 0)

    conv(NCH - 1, 0, 2)
    rs_mid(NCH - 1)
    conv(NCH - 1, 2, 2)

    @pl.loop(0, 4)
    def _(m):
        rows = pl.ds(pl.multiple_of(GROUP * m, GROUP), GROUP)
        total = jnp.zeros((GROUP, 128), F32)
        for pair in range(5):
            v = yacc[rows, 128 * pair : 128 * pair + 128]
            t0, t1 = 2 * pair, min(2 * pair + 1, 8)
            first = pltpu.roll(v, -DELTA[t0] % GROUP, 0)
            second = first if t1 == t0 else pltpu.roll(v, -DELTA[t1] % GROUP, 0)
            total += jnp.where(low4, first, second) * jnp.concatenate([maskc[pair]] * 4, axis=0)
        total += pltpu.roll(total, OWN, 1)
        for i in range(4):
            cs[4 * m + i] = total[SLOT * i : SLOT * i + WIRE]

    def c_pass(k):
        return remote(cs.at[2 * k + 1], cp.at[k], csend.at[8 + k], crecv.at[8 + k], partner)

    mycols = pl.ds(pl.multiple_of(128 * chip_of(0, 0), 128), 128)

    def c_copy(k):
        return remote(cf.at[k], out_ref.at[:, mycols], csend.at[k], crecv.at[INVERSE[k]], at(*rel[k]))

    def c_in(k):
        cols = pl.ds(pl.multiple_of(128 * chip_of(*rel[k]), 128), 128)
        return remote(cf.at[k], out_ref.at[:, cols], csend.at[k], crecv.at[k], at(*rel[k]))

    order = (4, 7, 1, 2, 5, 6, 3, 0)
    for k in order:
        c_pass(k).start()

    rs_end(NCH - 1)

    def unit(first, i):
        u = first + i
        t, j, h = lax.div(u, 8), lax.div(lax.rem(u, 8), 2), lax.rem(u, 2)
        return fin[j, h, t - lax.div(9 * y - j + 3, 4)]

    for i in range(9):
        zs[i] = unit(18 * y + 9 * (1 - zh), i)
    zcopy = remote(zs, zr, zsem.at[0], zsem.at[1], far)
    zcopy.start()

    mine = (lax.broadcasted_iota(jnp.int32, (WIRE, 128), 1) < OWN) == (core == 0)
    for k in order:
        c_pass(k).wait_recv()
        full = jnp.where(mine, cs[2 * k], cp[k])
        if k == 0:
            out_ref[:, mycols] = full
        else:
            cf[k] = full
            c_copy(k).start()

    zcopy.wait_recv()
    for i in range(9):
        fg_ref[:, 128 * i : 128 * (i + 1)] = unit(18 * y + 9 * zh, i) + zr[i]

    for k in range(1, 8):
        c_in(k).wait_recv()
    zcopy.wait_send()
    for k in range(8):
        if k > 0:
            grad_copy(k).wait_send()
            c_copy(k).wait_send()
        grad_pass(k).wait_send()
        c_pass(k).wait_send()

    @pl.loop(0, NCH)
    def _(j):
        for kind in range(NK):
            x_copy(j, kind).wait_send()
        for kind in range(6):
            r_copy(j, kind).wait_send()


def on_device(images, filters, out_grad):
    img, rows, cols, chans = images.shape
    x = jnp.pad(images.reshape(ROWS, chans), ((0, WIRE - ROWS), (0, 0)))
    g = jnp.pad(out_grad.reshape(ROWS, chans), ((0, WIRE - ROWS), (0, 0)))
    vmem = pl.BlockSpec(memory_space=pltpu.VMEM)
    dma = pltpu.SemaphoreType.DMA
    out, fg = pl.pallas_call(
        kernel,
        out_shape=(jax.ShapeDtypeStruct((WIRE, chans), F32), jax.ShapeDtypeStruct((OWN, 1152), F32)),
        in_specs=[vmem] * 3,
        out_specs=(vmem, vmem),
        scratch_shapes=[
            pltpu.VMEM((NCH, NSLOT, WIRE, CW), F32),
            pltpu.VMEM((NCH, TOTAL, 3 * CW), BF16),
            pltpu.VMEM((NCH, 3 * CW, 512), BF16),
            pltpu.VMEM((NCH, 2 * CW, 128), BF16),
            pltpu.VMEM((NSLOT, WIRE, 128), F32),
            pltpu.VMEM((640, TOTAL), BF16),
            pltpu.VMEM((640, TOTAL), BF16),
            pltpu.VMEM((5, SLOT, 128), F32),
            pltpu.VMEM((5, SLOT, 128), F32),
            pltpu.VMEM((TOTAL, 640), F32),
            pltpu.VMEM((NCH, 2, 10, OWN, 128), F32),
            pltpu.VMEM((NCH, 2, 3, OWN, 128), F32),
            pltpu.VMEM((NCH, 4, 3, OWN, 128), F32),
            pltpu.VMEM((NCH, 2, 3, OWN, 128), F32),
            pltpu.VMEM((NCH, 2, 3, OWN, 128), F32),
            pltpu.VMEM((9, OWN, 128), F32),
            pltpu.VMEM((9, OWN, 128), F32),
            pltpu.VMEM((NSLOT, WIRE, 128), F32),
            pltpu.VMEM((8, WIRE, 128), F32),
            pltpu.VMEM((8, WIRE, 128), F32),
            dma((NCH, NK)), dma((NCH, NK)),
            dma((16,)), dma((16,)),
            dma((16,)), dma((16,)),
            dma((NCH, 6)), dma((NCH, 6)),
            dma((2,)),
        ],
        compiler_params=pltpu.CompilerParams(
            collective_id=0, has_side_effects=True, vmem_limit_bytes=66_000_000
        ),
    )(x, filters.reshape(OWN, 9 * chans), g)
    return out[:ROWS].reshape(img, rows, cols, chans), fg[None]


def solution(mesh):
    return jax.shard_map(
        on_device,
        mesh=mesh,
        in_specs=(
            P(("replica", "shard"), None, None, None),
            P(None, "shard", None),
            P(("replica", "shard"), None, None, None),
        ),
        out_specs=(P(("replica", "shard"), None, None, None), P(None, "shard", "replica")),
        check_vma=False,
    )
```

```python
import functools

import jax
import jax.numpy as jnp
from jax import lax
from jax.experimental import pallas as pl
from jax.experimental.pallas import tpu as pltpu
from jax.sharding import PartitionSpec as P

MESH = pl.DeviceIdType.MESH
F32 = jnp.float32
BF16 = jnp.bfloat16
NX = 4
NY = 4
NCH = 4
CW = 256
ROWS = 147
WIRE = 152
SLOT = 160
CUT = 80
NSLOT = 16
TOTAL = SLOT * NSLOT
GROUP = 4 * SLOT
OWN = 64
DELTA = [7 * (t // 3 - 1) + (t % 3 - 1) for t in range(9)]

S_OWN, S_A, S_B, S_D, S_C, S_E, S_F, S_G = 0, 2, 4, 6, 8, 10, 12, 14
K_A, K_B, K_C, K_D1, K_D2, K_E, K_F, K_G1, K_G2, K_P = range(10)
NK = K_P + 8
INVERSE = [0, 2, 1, 3, 4, 6, 5, 7]


def kernel(
    x_hbm, f_hbm, g_hbm, out_ref, fg_ref,
    xin, gin, f_ref, x_ref, g_ref, xg, x3, f3t, f8t, gall, gsh, gsl, maskc, maskg, yacc, fgu, r1, r2, sy, fin, zs, zr, cs, cp, cf,
    xsend, xrecv, gsend, grecv, csend, crecv, rsend, rrecv, zsend, zrecv, isem,
):
    rep = lax.axis_index("replica")
    shard = lax.axis_index("shard")
    core = lax.rem(shard, 2)
    x = lax.rem(lax.div(shard, 2), NX)
    z = lax.div(shard, 2 * NX)
    y = lax.div(rep, 2)
    zh = lax.rem(rep, 2)

    def at(dx, dz, dc=0):
        xx = lax.rem(x + dx + NX, NX)
        zz = lax.rem(z + dz, 2)
        cc = lax.rem(core + dc, 2)
        return (rep, zz * 2 * NX + xx * 2 + cc)

    def chip_of(dx, dz):
        return lax.rem(z + dz, 2) * NX + lax.rem(x + dx + NX, NX)

    rel = [(0, 0), (-1, 0), (1, 0), (2, 0), (0, 1), (-1, 1), (1, 1), (2, 1)]
    partner = at(0, 0, 1)
    yp = lax.rem(y + 1, NY)
    ym = lax.rem(y + NY - 1, NY)
    y2 = lax.rem(y + 2, NY)
    up = (yp * 2 + zh, shard)
    down = (ym * 2 + zh, shard)
    far = (y * 2 + 1 - zh, shard)

    peers = [at(*rel[k]) for k in range(1, 8)] + [partner, up, down, far]
    barrier = pltpu.get_barrier_semaphore()
    for peer in peers:
        pl.semaphore_signal(barrier, inc=1, device_id=peer, device_id_type=MESH)

    loads = [
        pltpu.make_async_copy(src, dst, isem.at[i])
        for i, (src, dst) in enumerate(((x_hbm, xin), (g_hbm, gin), (f_hbm, f_ref)))
    ]
    for load in loads:
        load.start()
    for load, src, dst in ((loads[0], xin, x_ref), (loads[1], gin, g_ref)):
        load.wait()
        dst[144:WIRE] = jnp.zeros((WIRE - 144, dst.shape[1]), F32)
        for r in range(21):
            dst[7 * r : 7 * r + 7] = src[r // 7, r % 7]
    pl.semaphore_wait(barrier, len(peers))

    def remote(src, dst, ssem, rsem, dev):
        return pltpu.make_async_remote_copy(
            src_ref=src, dst_ref=dst, send_sem=ssem, recv_sem=rsem, device_id=dev, device_id_type=MESH
        )

    def grad_copy(k):
        if k == 0:
            return None
        cols = pl.ds(pl.multiple_of(128 * chip_of(*rel[k]), 128), 128)
        return remote(g_ref.at[:, cols], gall.at[2 * INVERSE[k]], gsend.at[k], grecv.at[INVERSE[k]], at(*rel[k]))

    def grad_in(k):
        return remote(gall.at[2 * k], gall.at[2 * k], gsend.at[k], grecv.at[k], at(*rel[k]))

    def grad_pass(k):
        if k == 0:
            cols = pl.ds(pl.multiple_of(128 * chip_of(0, 0), 128), 128)
            src = g_ref.at[:, cols]
        else:
            src = gall.at[2 * k]
        return remote(src, gall.at[2 * k + 1], gsend.at[8 + k], grecv.at[8 + k], partner)

    def own(j):
        return x_ref.at[:, pl.ds(pl.multiple_of(CW * j, CW), CW)]

    def x_copy(j, kind):
        lo, hi = pl.ds(0, CUT), pl.ds(CUT, WIRE - CUT)
        if kind >= K_P:
            k = kind - K_P
            src = own(j) if k == 0 else xg.at[j, 2 * k]
            dst, dev = xg.at[j, 2 * k + 1], partner
        elif kind == K_A:
            src, dst, dev = own(j), xg.at[j, S_A], at(1, 0)
        elif kind == K_B:
            src, dst, dev = own(j), xg.at[j, S_B], at(-1, 0)
        elif kind == K_C:
            src, dst, dev = own(j), xg.at[j, S_C], at(0, 1)
        elif kind == K_D1:
            src, dst, dev = xg.at[j, S_A, lo], xg.at[j, S_D, lo], at(1, 0)
        elif kind == K_D2:
            src, dst, dev = xg.at[j, S_B, hi], xg.at[j, S_D, hi], at(-1, 0)
        elif kind == K_E:
            src, dst, dev = xg.at[j, S_C], xg.at[j, S_E], at(1, 0)
        elif kind == K_F:
            src, dst, dev = xg.at[j, S_C], xg.at[j, S_F], at(-1, 0)
        elif kind == K_G1:
            src, dst, dev = xg.at[j, S_D, lo], xg.at[j, S_G, lo], at(0, 1)
        else:
            src, dst, dev = xg.at[j, S_D, hi], xg.at[j, S_G, hi], at(0, 1)
        return remote(src, dst, xsend.at[j, kind], xrecv.at[j, kind], dev)

    def x_own(j):
        for kind in (K_A, K_B, K_C, K_P):
            x_copy(j, kind).start()

    x_own(0)

    for j in range(NCH):
        xg[j, 0] = x_ref[:, CW * j : CW * (j + 1)]
    gall[0] = g_ref[:, pl.ds(pl.multiple_of(128 * chip_of(0, 0), 128), 128)]

    lane = lax.broadcasted_iota(jnp.int32, (SLOT, 128), 1)
    low = lane < OWN
    pos = lax.broadcasted_iota(jnp.int32, (SLOT, 128), 0).astype(F32)
    rem = pos - 49.0 * jnp.floor((pos + 0.5) * (1.0 / 49.0))
    hh = jnp.floor((rem + 0.5) * (1.0 / 7.0))
    ww = rem - 7.0 * hh
    for pair in range(5):
        t0, t1 = 2 * pair, min(2 * pair + 1, 8)
        da = jnp.where(low, float(t0 // 3 - 1), float(t1 // 3 - 1))
        dc = jnp.where(low, float(t0 % 3 - 1), float(t1 % 3 - 1))
        for sign, mask in ((1.0, maskc), (-1.0, maskg)):
            h1, w1 = hh + sign * da, ww + sign * dc
            inside = jnp.minimum(jnp.minimum(h1, 6.0 - h1), jnp.minimum(w1, 6.0 - w1)) > -0.5
            mask[pair] = jnp.where(inside, 1.0, 0.0)

    def halves(v):
        hi = v.astype(BF16)
        lo = (v - hi.astype(F32)).astype(BF16)
        return hi, lo

    loads[2].wait()

    @pl.loop(0, NCH)
    def _(j):
        for pair in range(4):
            parts = []
            for t in (2 * pair, 2 * pair + 1):
                parts.append(f_ref[:, pl.ds(pl.multiple_of(t * 1024 + CW * j, CW), CW)])
            hi, lo = halves(jnp.concatenate(parts, axis=0).T)
            cols = slice(128 * pair, 128 * pair + 128)
            f3t[j, 0:CW, cols] = hi
            f3t[j, CW : 2 * CW, cols] = hi
            f3t[j, 2 * CW : 3 * CW, cols] = lo
        f8 = f_ref[:, pl.ds(pl.multiple_of(8 * 1024 + CW * j, CW), CW)]
        hi8 = f8.astype(BF16).astype(F32)
        both = jnp.concatenate([hi8, f8 - hi8], axis=0).T.astype(BF16)
        f8t[j, 0:CW, :] = both
        f8t[j, CW : 2 * CW, :] = both

    lane4 = lax.broadcasted_iota(jnp.int32, (GROUP, 128), 1)
    low4 = lane4 < OWN
    mine4 = (lane4 < OWN) == (core == 0)

    def padded(v):
        return jnp.concatenate([v, jnp.zeros((SLOT - WIRE, v.shape[1]), v.dtype)], axis=0)

    def grad_start():
        for k in (3, 7, 1, 2, 5, 6, 4):
            grad_copy(k).start()
        grad_pass(0).start()

    def grad_forward():
        for k in (1, 2, 5, 6, 4, 3, 7):
            grad_in(k).wait_recv()
            grad_pass(k).start()

    def grad_wait():
        for k in range(8):
            grad_pass(k).wait_recv()

    def grad_stack():
        @pl.loop(0, 4)
        def _(m):
            g = jnp.concatenate([padded(gall[4 * m + i]) for i in range(4)], axis=0)
            gg = jnp.where(mine4, g, pltpu.roll(g, OWN, 1))
            cols = pl.ds(pl.multiple_of(GROUP * m, GROUP), GROUP)
            for pair in range(5):
                t0, t1 = 2 * pair, min(2 * pair + 1, 8)
                first = pltpu.roll(gg, DELTA[t0] % GROUP, 0)
                second = first if t1 == t0 else pltpu.roll(gg, DELTA[t1] % GROUP, 0)
                mask = jnp.concatenate([maskg[pair]] * 4, axis=0)
                hi, lo = halves((jnp.where(low4, first, second) * mask).T)
                gsh[128 * pair : 128 * pair + 128, cols] = hi
                gsl[128 * pair : 128 * pair + 128, cols] = lo

    def window(yy, j):
        return lax.div(9 * yy - j + 3, 4)

    def taps3(j, h, yy):
        return fgu[j, h, pl.ds(window(yy, j), 3)]

    R_OUT = (y2, y2, yp, ym, yp, ym)
    R_IN = (yp, ym, y, y, y, y)

    def r_copy(j, kind, part):
        span = pl.ds(2, 1) if part else pl.ds(0, 2)
        yy = R_OUT[kind]
        dev = down if kind in (1, 3, 5) else up
        if kind < 4:
            first = window(yy, j)
            src = fgu.at[j, (0, 1, 1, 0)[kind], pl.ds(first + 2, 1) if part else pl.ds(first, 2)]
        else:
            src = sy.at[j, kind - 4, span]
        dst = r1.at[j, kind, span] if kind < 2 else r2.at[j, (None, None, 1, 2, 0, 3)[kind], span]
        return remote(src, dst, rsend.at[j, kind, part], rrecv.at[j, kind, part], dev)

    def r_start(j, kind):
        r_copy(j, kind, 0).start()

        @pl.when(R_OUT[kind] == j)
        def _():
            r_copy(j, kind, 1).start()

    def r_recv(j, kind):
        r_copy(j, kind, 0).wait_recv()

        @pl.when(R_IN[kind] == j)
        def _():
            r_copy(j, kind, 1).wait_recv()

    def r_sent(j, kind):
        r_copy(j, kind, 0).wait_send()

        @pl.when(R_OUT[kind] == j)
        def _():
            r_copy(j, kind, 1).wait_send()

    def rs_mid(j):
        r_recv(j, 0)
        sy[j, 0] = taps3(j, 0, yp) + r1[j, 0]
        r_start(j, 4)
        r_recv(j, 1)
        sy[j, 1] = taps3(j, 1, ym) + r1[j, 1]
        r_start(j, 5)

    def rs_end(j):
        for kind in (2, 3, 4, 5):
            r_recv(j, kind)
        fin[j, 0] = taps3(j, 0, y) + r2[j, 0] + r2[j, 2]
        fin[j, 1] = taps3(j, 1, y) + r2[j, 1] + r2[j, 3]

    def nn(a, b):
        return lax.dot_general(a, b, (((1,), (0,)), ((), ())), preferred_element_type=F32)

    def unit_of(first, k):
        i = lax.rem(k - lax.rem(first, 8) + 8, 8) if k is not None else 8
        u = first + i
        t, j, h = lax.div(u, 8), lax.div(lax.rem(u, 8), 2), lax.rem(u, 2)
        return i, fin[j, h, t - lax.div(9 * y - j + 3, 4)]

    first_mine = 18 * y + 9 * zh
    first_far = 18 * y + 9 * (1 - zh)

    def z_copy(j, part):
        span = pl.ds(8, 1) if part else pl.ds(2 * j, 2)
        return remote(zs.at[span], zr.at[span], zsend.at[j, part], zrecv.at[j, part], far)

    def z_each(j, act):
        act(z_copy(j, 0))

        @pl.when(y == j)
        def _():
            act(z_copy(j, 1))

    def z_start(j):
        for h in range(2):
            zs[2 * j + h] = unit_of(first_far, 2 * j + h)[1]

        @pl.when(y == j)
        def _():
            zs[8] = unit_of(first_far, None)[1]

        z_each(j, lambda copy: copy.start())

    def conv_group(j, m):
        rows = pl.ds(pl.multiple_of(GROUP * m, GROUP), GROUP)
        main = nn(x3[j, rows, :], f3t[j])
        last = nn(x3[j, rows, 0 : 2 * CW], f8t[j])

        @pl.when(j == 0)
        def _():
            yacc[rows, 0:512] = main
            yacc[rows, 512:640] = last

        @pl.when(j > 0)
        def _():
            yacc[rows, 0:512] += main
            yacc[rows, 512:640] += last

    def to_partner(j, *slots):
        for s in slots:
            x_copy(j, K_P + s // 2).start()

    def hop_one(j):
        for kind in (K_A, K_B, K_C):
            x_copy(j, kind).wait_recv()
        for kind in (K_D1, K_D2, K_E, K_F):
            x_copy(j, kind).start()
        to_partner(j, S_A, S_B, S_C)

    def hop_two(j):
        x_copy(j, K_D1).wait_recv()
        x_copy(j, K_G1).start()
        x_copy(j, K_D2).wait_recv()
        x_copy(j, K_G2).start()
        to_partner(j, S_D)

    def hop_three(j):
        x_copy(j, K_E).wait_recv()
        x_copy(j, K_F).wait_recv()
        to_partner(j, S_E, S_F)

    def arrive_far(j):
        x_copy(j, K_G1).wait_recv()
        x_copy(j, K_G2).wait_recv()
        to_partner(j, S_G)

    def convert(j, half):
        for k in range(4 * half, 4 * half + 4):
            x_copy(j, K_P + k).wait_recv()

        @pl.loop(8 * half, 8 * half + 8)
        def _(s):
            hi, lo = halves(padded(xg[j, s]))
            rows = pl.ds(pl.multiple_of(SLOT * s, SLOT), SLOT)
            x3[j, rows, 0:CW] = hi
            x3[j, rows, CW : 2 * CW] = lo
            x3[j, rows, 2 * CW : 3 * CW] = hi

    def filter_grad(j):
        res = nn(gsh[0:576, :], x3[j, :, 0:CW])
        res += nn(gsl[0:576, :], x3[j, :, 0:CW])
        res += nn(gsh[0:576, :], x3[j, :, CW : 2 * CW])
        for h in range(2):
            for t in range(9):
                fgu[j, h, t] = res[OWN * t : OWN * (t + 1), 128 * h : 128 * (h + 1)]
            fgu[j, h, 9] = jnp.zeros((OWN, 128), F32)

    def rs_start(j, kind):
        r_start(j, kind)
        r_start(j, kind + 1)

    def tap_sum(m):
        rows = pl.ds(pl.multiple_of(GROUP * m, GROUP), GROUP)
        total = jnp.zeros((GROUP, 128), F32)
        for pair in range(5):
            v = yacc[rows, 128 * pair : 128 * pair + 128]
            t0, t1 = 2 * pair, min(2 * pair + 1, 8)
            first = pltpu.roll(v, -DELTA[t0] % GROUP, 0)
            second = first if t1 == t0 else pltpu.roll(v, -DELTA[t1] % GROUP, 0)
            total += jnp.where(low4, first, second) * jnp.concatenate([maskc[pair]] * 4, axis=0)
        total += pltpu.roll(total, OWN, 1)
        for i in range(4):
            cs[4 * m + i] = total[SLOT * i : SLOT * i + WIRE]

    def c_pass(k):
        return remote(cs.at[2 * k + 1], cp.at[k], csend.at[8 + k], crecv.at[8 + k], partner)

    mycols = pl.ds(pl.multiple_of(128 * chip_of(0, 0), 128), 128)

    def c_copy(k):
        return remote(cf.at[k], out_ref.at[:, mycols], csend.at[k], crecv.at[INVERSE[k]], at(*rel[k]))

    def c_in(k):
        cols = pl.ds(pl.multiple_of(128 * chip_of(*rel[k]), 128), 128)
        return remote(cf.at[k], out_ref.at[:, cols], csend.at[k], crecv.at[k], at(*rel[k]))

    def c_pass_group(m):
        for i in range(2):
            k = 2 * m + i
            remote(cs.at[2 * k + 1], cp.at[k], csend.at[8 + k], crecv.at[8 + k], partner).start()

    mine = (lax.broadcasted_iota(jnp.int32, (WIRE, 128), 1) < OWN) == (core == 0)

    def conv_send(m):
        for k in (2 * m, 2 * m + 1):
            c_pass(k).wait_recv()
            full = jnp.where(mine, cs[2 * k], cp[k])
            if k == 0:
                out_ref[:, mycols] = full
            else:
                cf[k] = full
                c_copy(k).start()

    hop_one(0)
    x_own(1)
    grad_start()
    hop_two(0)
    hop_three(0)
    arrive_far(0)
    convert(0, 0)
    convert(0, 1)

    @pl.loop(0, 16)
    def _(n):
        chunk = lax.div(n, 4)
        group = jnp.where((n == 8) | (n == 9), n - 8, jnp.where((n == 10) | (n == 11), n - 8, 3 - lax.rem(n, 4)))

        @pl.when(n == 1)
        def _():
            hop_one(1)
            x_own(2)

        @pl.when(n == 4)
        def _():
            grad_forward()
            hop_two(1)
            x_own(3)
            grad_wait()
            grad_stack()
            hop_three(1)
            arrive_far(1)

        @pl.when(n == 6)
        def _():
            hop_one(3)

        @pl.when(n == 7)
        def _():
            hop_two(2)

        @pl.when(n == 8)
        def _():
            hop_three(2)
            convert(2, 0)

        @pl.when(n == 9)
        def _():
            hop_two(3)

        @pl.when(n == 10)
        def _():
            convert(2, 1)

        @pl.when(n == 12)
        def _():
            rs_end(1)
            z_start(1)
            convert(3, 0)
            convert(3, 1)

        @pl.when((n == 4) | (n == 7) | (n == 10) | (n == 12))
        def _():
            c = jnp.where(n == 4, 0, jnp.where(n == 7, 1, jnp.where(n == 10, 2, 3)))

            @pl.when(c == 2)
            def _():
                rs_mid(1)

            filter_grad(c)
            rs_start(c, 0)

            @pl.when((c == 1) | (c == 3))
            def _():
                rs_mid(c - 1)

            rs_start(c, 2)

            @pl.when(c == 2)
            def _():
                rs_end(0)
                z_start(0)

        @pl.when(n == 4)
        def _():
            convert(1, 0)
            hop_one(2)
            convert(1, 1)

        @pl.when(n == 10)
        def _():
            hop_three(3)

        conv_group(chunk, group)

        @pl.when(n == 8)
        def _():
            arrive_far(2)

        @pl.when(n == 10)
        def _():
            arrive_far(3)

        @pl.when(n > 11)
        def _():
            done = 15 - n
            tap_sum(done)
            c_pass_group(done)

            for i in range(1, 4):

                @pl.when(done == 3 - i)
                def _():
                    conv_send(4 - i)
                    if i == 1:
                        rs_mid(NCH - 1)
                    if i == 2:
                        rs_end(NCH - 2)
                        z_start(NCH - 2)

    conv_send(0)
    rs_end(NCH - 1)
    z_start(NCH - 1)

    def z_wait(j):
        z_each(j, lambda copy: copy.wait_recv())

    for j in range(NCH):
        z_wait(j)

    def fg_out():
        for k in range(8):
            i, v = unit_of(first_mine, k)
            fg_ref[:, pl.ds(pl.multiple_of(128 * i, 128), 128)] = v + zr[k]
        fg_ref[:, 1024:1152] = unit_of(first_mine, None)[1] + zr[8]

    fg_out()

    def c_wait(k):
        c_in(k).wait_recv()

    for k in range(1, 8):
        c_wait(k)

    def drain():
        for k in range(8):
            if k > 0:
                grad_copy(k).wait_send()
                c_copy(k).wait_send()
            grad_pass(k).wait_send()
            c_pass(k).wait_send()
        for j in range(NCH):
            z_each(j, lambda copy: copy.wait_send())

        @pl.loop(0, NCH)
        def _(j):
            for kind in range(NK):
                x_copy(j, kind).wait_send()
            for kind in range(6):
                r_sent(j, kind)

    drain()


def on_device(images, filters, out_grad):
    img, rows, cols, chans = images.shape
    hbm = pl.BlockSpec(memory_space=pltpu.HBM)
    vmem = pl.BlockSpec(memory_space=pltpu.VMEM)
    dma = pltpu.SemaphoreType.DMA
    out, fg = pl.pallas_call(
        kernel,
        out_shape=(jax.ShapeDtypeStruct((WIRE, chans), F32), jax.ShapeDtypeStruct((OWN, 1152), F32)),
        in_specs=[hbm] * 3,
        out_specs=(vmem, vmem),
        scratch_shapes=[
            pltpu.VMEM(images.shape, F32),
            pltpu.VMEM(out_grad.shape, F32),
            pltpu.VMEM((OWN, 9 * chans), F32),
            pltpu.VMEM((WIRE, chans), F32),
            pltpu.VMEM((WIRE, chans), F32),
            pltpu.VMEM((NCH, NSLOT, WIRE, CW), F32),
            pltpu.VMEM((NCH, TOTAL, 3 * CW), BF16),
            pltpu.VMEM((NCH, 3 * CW, 512), BF16),
            pltpu.VMEM((NCH, 2 * CW, 128), BF16),
            pltpu.VMEM((NSLOT, WIRE, 128), F32),
            pltpu.VMEM((640, TOTAL), BF16),
            pltpu.VMEM((640, TOTAL), BF16),
            pltpu.VMEM((5, SLOT, 128), F32),
            pltpu.VMEM((5, SLOT, 128), F32),
            pltpu.VMEM((TOTAL, 640), F32),
            pltpu.VMEM((NCH, 2, 10, OWN, 128), F32),
            pltpu.VMEM((NCH, 2, 3, OWN, 128), F32),
            pltpu.VMEM((NCH, 4, 3, OWN, 128), F32),
            pltpu.VMEM((NCH, 2, 3, OWN, 128), F32),
            pltpu.VMEM((NCH, 2, 3, OWN, 128), F32),
            pltpu.VMEM((9, OWN, 128), F32),
            pltpu.VMEM((9, OWN, 128), F32),
            pltpu.VMEM((NSLOT, WIRE, 128), F32),
            pltpu.VMEM((8, WIRE, 128), F32),
            pltpu.VMEM((8, WIRE, 128), F32),
            dma((NCH, NK)), dma((NCH, NK)),
            dma((16,)), dma((16,)),
            dma((16,)), dma((16,)),
            dma((NCH, 6, 2)), dma((NCH, 6, 2)),
            dma((NCH, 2)), dma((NCH, 2)),
            dma((3,)),
        ],
        compiler_params=pltpu.CompilerParams(
            collective_id=0, has_side_effects=True, vmem_limit_bytes=66_000_000
        ),
    )(images, filters.reshape(OWN, 9 * chans), out_grad)
    return out[:ROWS].reshape(img, rows, cols, chans), fg[None]


def solution(mesh):
    return jax.shard_map(
        on_device,
        mesh=mesh,
        in_specs=(
            P(("replica", "shard"), None, None, None),
            P(None, "shard", None),
            P(("replica", "shard"), None, None, None),
        ),
        out_specs=(P(("replica", "shard"), None, None, None), P(None, "shard", "replica")),
        check_vma=False,
    )
```

```python
import functools

import jax
import jax.numpy as jnp
from jax import lax
from jax.experimental import pallas as pl
from jax.experimental.pallas import tpu as pltpu
from jax.sharding import PartitionSpec as P

MESH = pl.DeviceIdType.MESH
F32 = jnp.float32
BF16 = jnp.bfloat16
NX = 4
NY = 4
NCH = 4
CW = 256
ROWS = 147
WIRE = 152
SLOT = 160
CUT = 80
NSLOT = 16
TOTAL = SLOT * NSLOT
GROUP = 4 * SLOT
OWN = 64
DELTA = [7 * (t // 3 - 1) + (t % 3 - 1) for t in range(9)]

S_OWN, S_A, S_B, S_D, S_C, S_E, S_F, S_G = 0, 2, 4, 6, 8, 10, 12, 14
K_A, K_B, K_C, K_D1, K_D2, K_E, K_F, K_G1, K_G2, K_P = range(10)
NK = K_P + 8
INVERSE = [0, 2, 1, 3, 4, 6, 5, 7]


def kernel(
    x_hbm, f_hbm, g_hbm, out_ref, fg_ref,
    xin, gin, f_ref, x_ref, g_ref, xg, x3, f3t, f8t, gall, gsh, gsl, maskc, maskg, yacc, fgu, r1, r2, sy, fin, zs, zr, cs, cp, cf,
    xsend, xrecv, gsend, grecv, csend, crecv, rsend, rrecv, zsend, zrecv, isem,
):
    rep = lax.axis_index("replica")
    shard = lax.axis_index("shard")
    core = lax.rem(shard, 2)
    x = lax.rem(lax.div(shard, 2), NX)
    z = lax.div(shard, 2 * NX)
    y = lax.div(rep, 2)
    zh = lax.rem(rep, 2)

    def at(dx, dz, dc=0):
        xx = lax.rem(x + dx + NX, NX)
        zz = lax.rem(z + dz, 2)
        cc = lax.rem(core + dc, 2)
        return (rep, zz * 2 * NX + xx * 2 + cc)

    def chip_of(dx, dz):
        return lax.rem(z + dz, 2) * NX + lax.rem(x + dx + NX, NX)

    rel = [(0, 0), (-1, 0), (1, 0), (2, 0), (0, 1), (-1, 1), (1, 1), (2, 1)]
    partner = at(0, 0, 1)
    yp = lax.rem(y + 1, NY)
    ym = lax.rem(y + NY - 1, NY)
    y2 = lax.rem(y + 2, NY)
    up = (yp * 2 + zh, shard)
    down = (ym * 2 + zh, shard)
    far = (y * 2 + 1 - zh, shard)

    peers = [at(*rel[k]) for k in range(1, 8)] + [partner, up, down, far]
    barrier = pltpu.get_barrier_semaphore()
    for peer in peers:
        pl.semaphore_signal(barrier, inc=1, device_id=peer, device_id_type=MESH)

    loads = [
        pltpu.make_async_copy(src, dst, isem.at[i])
        for i, (src, dst) in enumerate(((x_hbm, xin), (g_hbm, gin), (f_hbm, f_ref)))
    ]
    for load in loads:
        load.start()

    def relayout(load, src, dst):
        load.wait()
        dst[144:WIRE] = jnp.zeros((WIRE - 144, dst.shape[1]), F32)
        for r in range(21):
            dst[7 * r : 7 * r + 7] = src[r // 7, r % 7]

    relayout(loads[0], xin, x_ref)
    pl.semaphore_wait(barrier, len(peers))

    def remote(src, dst, ssem, rsem, dev):
        return pltpu.make_async_remote_copy(
            src_ref=src, dst_ref=dst, send_sem=ssem, recv_sem=rsem, device_id=dev, device_id_type=MESH
        )

    def grad_copy(k):
        if k == 0:
            return None
        cols = pl.ds(pl.multiple_of(128 * chip_of(*rel[k]), 128), 128)
        return remote(g_ref.at[:, cols], gall.at[2 * INVERSE[k]], gsend.at[k], grecv.at[INVERSE[k]], at(*rel[k]))

    def grad_in(k):
        return remote(gall.at[2 * k], gall.at[2 * k], gsend.at[k], grecv.at[k], at(*rel[k]))

    def grad_pass(k):
        if k == 0:
            cols = pl.ds(pl.multiple_of(128 * chip_of(0, 0), 128), 128)
            src = g_ref.at[:, cols]
        else:
            src = gall.at[2 * k]
        return remote(src, gall.at[2 * k + 1], gsend.at[8 + k], grecv.at[8 + k], partner)

    def own(j):
        return x_ref.at[:, pl.ds(pl.multiple_of(CW * j, CW), CW)]

    def x_copy(j, kind):
        lo, hi = pl.ds(0, CUT), pl.ds(CUT, WIRE - CUT)
        if kind >= K_P:
            k = kind - K_P
            src = own(j) if k == 0 else xg.at[j, 2 * k]
            dst, dev = xg.at[j, 2 * k + 1], partner
        elif kind == K_A:
            src, dst, dev = own(j), xg.at[j, S_A], at(1, 0)
        elif kind == K_B:
            src, dst, dev = own(j), xg.at[j, S_B], at(-1, 0)
        elif kind == K_C:
            src, dst, dev = own(j), xg.at[j, S_C], at(0, 1)
        elif kind == K_D1:
            src, dst, dev = xg.at[j, S_A, lo], xg.at[j, S_D, lo], at(1, 0)
        elif kind == K_D2:
            src, dst, dev = xg.at[j, S_B, hi], xg.at[j, S_D, hi], at(-1, 0)
        elif kind == K_E:
            src, dst, dev = xg.at[j, S_C], xg.at[j, S_E], at(1, 0)
        elif kind == K_F:
            src, dst, dev = xg.at[j, S_C], xg.at[j, S_F], at(-1, 0)
        elif kind == K_G1:
            src, dst, dev = xg.at[j, S_D, lo], xg.at[j, S_G, lo], at(0, 1)
        else:
            src, dst, dev = xg.at[j, S_D, hi], xg.at[j, S_G, hi], at(0, 1)
        return remote(src, dst, xsend.at[j, kind], xrecv.at[j, kind], dev)

    def x_own(j):
        for kind in (K_A, K_B, K_C, K_P):
            x_copy(j, kind).start()

    x_own(0)
    relayout(loads[1], gin, g_ref)

    for j in range(NCH):
        xg[j, 0] = x_ref[:, CW * j : CW * (j + 1)]
    gall[0] = g_ref[:, pl.ds(pl.multiple_of(128 * chip_of(0, 0), 128), 128)]

    @pl.loop(0, NSLOT)
    def _(s):
        yacc[pl.ds(pl.multiple_of(SLOT * s, SLOT), SLOT), :] = jnp.zeros((SLOT, 640), F32)

    lane = lax.broadcasted_iota(jnp.int32, (SLOT, 128), 1)
    low = lane < OWN
    pos = lax.broadcasted_iota(jnp.int32, (SLOT, 128), 0).astype(F32)
    rem = pos - 49.0 * jnp.floor((pos + 0.5) * (1.0 / 49.0))
    hh = jnp.floor((rem + 0.5) * (1.0 / 7.0))
    ww = rem - 7.0 * hh
    for pair in range(5):
        t0, t1 = 2 * pair, min(2 * pair + 1, 8)
        da = jnp.where(low, float(t0 // 3 - 1), float(t1 // 3 - 1))
        dc = jnp.where(low, float(t0 % 3 - 1), float(t1 % 3 - 1))
        for sign, mask in ((1.0, maskc), (-1.0, maskg)):
            h1, w1 = hh + sign * da, ww + sign * dc
            inside = jnp.minimum(jnp.minimum(h1, 6.0 - h1), jnp.minimum(w1, 6.0 - w1)) > -0.5
            mask[pair] = jnp.where(inside, 1.0, 0.0)

    def halves(v):
        hi = v.astype(BF16)
        lo = (v - hi.astype(F32)).astype(BF16)
        return hi, lo

    loads[2].wait()

    @pl.loop(0, NCH)
    def _(j):
        for pair in range(4):
            parts = []
            for t in (2 * pair, 2 * pair + 1):
                parts.append(f_ref[:, pl.ds(pl.multiple_of(t * 1024 + CW * j, CW), CW)])
            hi, lo = halves(jnp.concatenate(parts, axis=0).T)
            cols = slice(128 * pair, 128 * pair + 128)
            f3t[j, 0:CW, cols] = hi
            f3t[j, CW : 2 * CW, cols] = hi
            f3t[j, 2 * CW : 3 * CW, cols] = lo
        f8 = f_ref[:, pl.ds(pl.multiple_of(8 * 1024 + CW * j, CW), CW)]
        hi8 = f8.astype(BF16).astype(F32)
        both = jnp.concatenate([hi8, f8 - hi8], axis=0).T.astype(BF16)
        f8t[j, 0:CW, :] = both
        f8t[j, CW : 2 * CW, :] = both

    lane4 = lax.broadcasted_iota(jnp.int32, (GROUP, 128), 1)
    low4 = lane4 < OWN
    mine4 = (lane4 < OWN) == (core == 0)

    def padded(v):
        return jnp.concatenate([v, jnp.zeros((SLOT - WIRE, v.shape[1]), v.dtype)], axis=0)

    def grad_start():
        for k in (3, 7, 1, 2, 5, 6, 4):
            grad_copy(k).start()
        grad_pass(0).start()

    def grad_forward():
        for k in (1, 2, 5, 6, 4, 3, 7):
            grad_in(k).wait_recv()
            grad_pass(k).start()

    def grad_wait():
        for k in range(8):
            grad_pass(k).wait_recv()

    def grad_stack():
        @pl.loop(0, 4)
        def _(m):
            g = jnp.concatenate([padded(gall[4 * m + i]) for i in range(4)], axis=0)
            gg = jnp.where(mine4, g, pltpu.roll(g, OWN, 1))
            cols = pl.ds(pl.multiple_of(GROUP * m, GROUP), GROUP)
            for pair in range(5):
                t0, t1 = 2 * pair, min(2 * pair + 1, 8)
                first = pltpu.roll(gg, DELTA[t0] % GROUP, 0)
                second = first if t1 == t0 else pltpu.roll(gg, DELTA[t1] % GROUP, 0)
                mask = jnp.concatenate([maskg[pair]] * 4, axis=0)
                hi, lo = halves((jnp.where(low4, first, second) * mask).T)
                gsh[128 * pair : 128 * pair + 128, cols] = hi
                gsl[128 * pair : 128 * pair + 128, cols] = lo

    def window(yy, j):
        return lax.div(9 * yy - j + 3, 4)

    def taps3(j, h, yy):
        return fgu[j, h, pl.ds(window(yy, j), 3)]

    R_OUT = (y2, y2, yp, ym, yp, ym)
    R_IN = (yp, ym, y, y, y, y)

    def r_copy(j, kind, part):
        span = pl.ds(2, 1) if part else pl.ds(0, 2)
        yy = R_OUT[kind]
        dev = down if kind in (1, 3, 5) else up
        if kind < 4:
            first = window(yy, j)
            src = fgu.at[j, (0, 1, 1, 0)[kind], pl.ds(first + 2, 1) if part else pl.ds(first, 2)]
        else:
            src = sy.at[j, kind - 4, span]
        dst = r1.at[j, kind, span] if kind < 2 else r2.at[j, (None, None, 1, 2, 0, 3)[kind], span]
        return remote(src, dst, rsend.at[j, kind, part], rrecv.at[j, kind, part], dev)

    def r_start(j, kind):
        r_copy(j, kind, 0).start()

        @pl.when(R_OUT[kind] == j)
        def _():
            r_copy(j, kind, 1).start()

    def r_recv(j, kind):
        r_copy(j, kind, 0).wait_recv()

        @pl.when(R_IN[kind] == j)
        def _():
            r_copy(j, kind, 1).wait_recv()

    def r_sent(j, kind):
        r_copy(j, kind, 0).wait_send()

        @pl.when(R_OUT[kind] == j)
        def _():
            r_copy(j, kind, 1).wait_send()

    def rs_mid(j):
        r_recv(j, 0)
        sy[j, 0] = taps3(j, 0, yp) + r1[j, 0]
        r_start(j, 4)
        r_recv(j, 1)
        sy[j, 1] = taps3(j, 1, ym) + r1[j, 1]
        r_start(j, 5)

    def rs_end(j):
        for kind in (2, 3, 4, 5):
            r_recv(j, kind)
        fin[j, 0] = taps3(j, 0, y) + r2[j, 0] + r2[j, 2]
        fin[j, 1] = taps3(j, 1, y) + r2[j, 1] + r2[j, 3]

    def nn(a, b):
        return lax.dot_general(a, b, (((1,), (0,)), ((), ())), preferred_element_type=F32)

    def unit_of(first, k):
        i = lax.rem(k - lax.rem(first, 8) + 8, 8) if k is not None else 8
        u = first + i
        t, j, h = lax.div(u, 8), lax.div(lax.rem(u, 8), 2), lax.rem(u, 2)
        return i, fin[j, h, t - lax.div(9 * y - j + 3, 4)]

    first_mine = 18 * y + 9 * zh
    first_far = 18 * y + 9 * (1 - zh)

    def z_copy(j, part):
        span = pl.ds(8, 1) if part else pl.ds(2 * j, 2)
        return remote(zs.at[span], zr.at[span], zsend.at[j, part], zrecv.at[j, part], far)

    def z_each(j, act):
        act(z_copy(j, 0))

        @pl.when(y == j)
        def _():
            act(z_copy(j, 1))

    def z_start(j):
        for h in range(2):
            zs[2 * j + h] = unit_of(first_far, 2 * j + h)[1]

        @pl.when(y == j)
        def _():
            zs[8] = unit_of(first_far, None)[1]

        z_each(j, lambda copy: copy.start())

    def conv_group(j, m):
        rows = pl.ds(pl.multiple_of(GROUP * m, GROUP), GROUP)
        main = nn(x3[j, rows, :], f3t[j])
        last = nn(x3[j, rows, 0 : 2 * CW], f8t[j])
        yacc[rows, 0:512] += main
        yacc[rows, 512:640] += last

    def to_partner(j, *slots):
        for s in slots:
            x_copy(j, K_P + s // 2).start()

    def hop_one(j):
        for kind in (K_A, K_B, K_C):
            x_copy(j, kind).wait_recv()
        for kind in (K_D1, K_D2, K_E, K_F):
            x_copy(j, kind).start()
        to_partner(j, S_A, S_B, S_C)

    def hop_two(j):
        x_copy(j, K_D1).wait_recv()
        x_copy(j, K_G1).start()
        x_copy(j, K_D2).wait_recv()
        x_copy(j, K_G2).start()
        to_partner(j, S_D)

    def hop_three(j):
        x_copy(j, K_E).wait_recv()
        x_copy(j, K_F).wait_recv()
        to_partner(j, S_E, S_F)

    def arrive_far(j):
        x_copy(j, K_G1).wait_recv()
        x_copy(j, K_G2).wait_recv()
        to_partner(j, S_G)

    def convert(j, half):
        for k in range(4 * half, 4 * half + 4):
            x_copy(j, K_P + k).wait_recv()

        @pl.loop(8 * half, 8 * half + 8)
        def _(s):
            hi, lo = halves(padded(xg[j, s]))
            rows = pl.ds(pl.multiple_of(SLOT * s, SLOT), SLOT)
            x3[j, rows, 0:CW] = hi
            x3[j, rows, CW : 2 * CW] = lo
            x3[j, rows, 2 * CW : 3 * CW] = hi

    def filter_grad(j):
        res = nn(gsh[0:576, :], x3[j, :, 0:CW])
        res += nn(gsl[0:576, :], x3[j, :, 0:CW])
        res += nn(gsh[0:576, :], x3[j, :, CW : 2 * CW])
        for h in range(2):
            for t in range(9):
                fgu[j, h, t] = res[OWN * t : OWN * (t + 1), 128 * h : 128 * (h + 1)]
            fgu[j, h, 9] = jnp.zeros((OWN, 128), F32)

    def rs_start(j, kind):
        r_start(j, kind)
        r_start(j, kind + 1)

    def tap_sum(m):
        rows = pl.ds(pl.multiple_of(GROUP * m, GROUP), GROUP)
        total = jnp.zeros((GROUP, 128), F32)
        for pair in range(5):
            v = yacc[rows, 128 * pair : 128 * pair + 128]
            t0, t1 = 2 * pair, min(2 * pair + 1, 8)
            first = pltpu.roll(v, -DELTA[t0] % GROUP, 0)
            second = first if t1 == t0 else pltpu.roll(v, -DELTA[t1] % GROUP, 0)
            total += jnp.where(low4, first, second) * jnp.concatenate([maskc[pair]] * 4, axis=0)
        total += pltpu.roll(total, OWN, 1)
        for i in range(4):
            cs[4 * m + i] = total[SLOT * i : SLOT * i + WIRE]

    def c_pass(k):
        return remote(cs.at[2 * k + 1], cp.at[k], csend.at[8 + k], crecv.at[8 + k], partner)

    mycols = pl.ds(pl.multiple_of(128 * chip_of(0, 0), 128), 128)

    def c_copy(k):
        return remote(cf.at[k], out_ref.at[:, mycols], csend.at[k], crecv.at[INVERSE[k]], at(*rel[k]))

    def c_in(k):
        cols = pl.ds(pl.multiple_of(128 * chip_of(*rel[k]), 128), 128)
        return remote(cf.at[k], out_ref.at[:, cols], csend.at[k], crecv.at[k], at(*rel[k]))

    def c_pass_group(m):
        for i in range(2):
            k = 2 * m + i
            remote(cs.at[2 * k + 1], cp.at[k], csend.at[8 + k], crecv.at[8 + k], partner).start()

    mine = (lax.broadcasted_iota(jnp.int32, (WIRE, 128), 1) < OWN) == (core == 0)

    def conv_send(m):
        for k in (2 * m, 2 * m + 1):
            c_pass(k).wait_recv()
            full = jnp.where(mine, cs[2 * k], cp[k])
            if k == 0:
                out_ref[:, mycols] = full
            else:
                cf[k] = full
                c_copy(k).start()

    hop_one(0)
    x_own(1)
    grad_start()
    hop_two(0)
    hop_three(0)
    arrive_far(0)
    convert(0, 0)
    convert(0, 1)

    @pl.loop(0, 16)
    def _(n):
        chunk = lax.div(n, 4)
        group = jnp.where((n == 8) | (n == 9), n - 8, jnp.where((n == 10) | (n == 11), n - 8, 3 - lax.rem(n, 4)))

        @pl.when(n == 1)
        def _():
            hop_one(1)
            x_own(2)

        @pl.when(n == 4)
        def _():
            grad_forward()
            hop_two(1)
            x_own(3)
            grad_wait()
            grad_stack()
            hop_three(1)
            arrive_far(1)

        @pl.when(n == 6)
        def _():
            hop_one(3)

        @pl.when(n == 7)
        def _():
            hop_two(2)

        @pl.when(n == 8)
        def _():
            hop_three(2)
            convert(2, 0)

        @pl.when(n == 9)
        def _():
            hop_two(3)

        @pl.when(n == 10)
        def _():
            convert(2, 1)

        @pl.when(n == 12)
        def _():
            rs_end(1)
            z_start(1)
            convert(3, 0)
            convert(3, 1)

        @pl.when((n == 4) | (n == 7) | (n == 10) | (n == 13))
        def _():
            c = jnp.where(n == 4, 0, jnp.where(n == 7, 1, jnp.where(n == 10, 2, 3)))

            @pl.when(c > 1)
            def _():
                rs_mid(c - 1)

            @pl.when(c == 3)
            def _():
                conv_send(3)

            filter_grad(c)
            rs_start(c, 0)

            @pl.when(c == 1)
            def _():
                rs_mid(0)

            rs_start(c, 2)

            @pl.when(c == 2)
            def _():
                rs_end(0)
                z_start(0)

        @pl.when(n == 4)
        def _():
            convert(1, 0)
            hop_one(2)
            convert(1, 1)

        @pl.when(n == 10)
        def _():
            hop_three(3)

        conv_group(chunk, group)

        @pl.when(n == 8)
        def _():
            arrive_far(2)

        @pl.when(n == 10)
        def _():
            arrive_far(3)

        @pl.when(n > 11)
        def _():
            done = 15 - n
            tap_sum(done)
            c_pass_group(done)

            @pl.when(n == 14)
            def _():
                conv_send(2)
                rs_end(NCH - 2)
                z_start(NCH - 2)

            @pl.when(n == 15)
            def _():
                rs_mid(NCH - 1)
                conv_send(1)

    conv_send(0)
    rs_end(NCH - 1)
    z_start(NCH - 1)

    def z_wait(j):
        z_each(j, lambda copy: copy.wait_recv())

    for j in range(NCH):
        z_wait(j)

    def fg_out():
        for k in range(8):
            i, v = unit_of(first_mine, k)
            fg_ref[:, pl.ds(pl.multiple_of(128 * i, 128), 128)] = v + zr[k]
        fg_ref[:, 1024:1152] = unit_of(first_mine, None)[1] + zr[8]

    fg_out()

    def c_wait(k):
        c_in(k).wait_recv()

    for k in range(1, 8):
        c_wait(k)

    def drain():
        for k in range(8):
            if k > 0:
                grad_copy(k).wait_send()
                c_copy(k).wait_send()
            grad_pass(k).wait_send()
            c_pass(k).wait_send()
        for j in range(NCH):
            z_each(j, lambda copy: copy.wait_send())

        @pl.loop(0, NCH)
        def _(j):
            for kind in range(NK):
                x_copy(j, kind).wait_send()
            for kind in range(6):
                r_sent(j, kind)

    drain()


def finish(o_ref, f_ref, out_ref, fg_ref):
    for r in range(21):
        out_ref[r // 7, r % 7] = o_ref[7 * r : 7 * r + 7]
    fg_ref[0] = f_ref[...]


def on_device(images, filters, out_grad):
    img, rows, cols, chans = images.shape
    hbm = pl.BlockSpec(memory_space=pltpu.HBM)
    vmem = pl.BlockSpec(memory_space=pltpu.VMEM)
    dma = pltpu.SemaphoreType.DMA
    out, fg = pl.pallas_call(
        kernel,
        out_shape=(jax.ShapeDtypeStruct((WIRE, chans), F32), jax.ShapeDtypeStruct((OWN, 1152), F32)),
        in_specs=[hbm] * 3,
        out_specs=(vmem, vmem),
        scratch_shapes=[
            pltpu.VMEM(images.shape, F32),
            pltpu.VMEM(out_grad.shape, F32),
            pltpu.VMEM((OWN, 9 * chans), F32),
            pltpu.VMEM((WIRE, chans), F32),
            pltpu.VMEM((WIRE, chans), F32),
            pltpu.VMEM((NCH, NSLOT, WIRE, CW), F32),
            pltpu.VMEM((NCH, TOTAL, 3 * CW), BF16),
            pltpu.VMEM((NCH, 3 * CW, 512), BF16),
            pltpu.VMEM((NCH, 2 * CW, 128), BF16),
            pltpu.VMEM((NSLOT, WIRE, 128), F32),
            pltpu.VMEM((640, TOTAL), BF16),
            pltpu.VMEM((640, TOTAL), BF16),
            pltpu.VMEM((5, SLOT, 128), F32),
            pltpu.VMEM((5, SLOT, 128), F32),
            pltpu.VMEM((TOTAL, 640), F32),
            pltpu.VMEM((NCH, 2, 10, OWN, 128), F32),
            pltpu.VMEM((NCH, 2, 3, OWN, 128), F32),
            pltpu.VMEM((NCH, 4, 3, OWN, 128), F32),
            pltpu.VMEM((NCH, 2, 3, OWN, 128), F32),
            pltpu.VMEM((NCH, 2, 3, OWN, 128), F32),
            pltpu.VMEM((9, OWN, 128), F32),
            pltpu.VMEM((9, OWN, 128), F32),
            pltpu.VMEM((NSLOT, WIRE, 128), F32),
            pltpu.VMEM((8, WIRE, 128), F32),
            pltpu.VMEM((8, WIRE, 128), F32),
            dma((NCH, NK)), dma((NCH, NK)),
            dma((16,)), dma((16,)),
            dma((16,)), dma((16,)),
            dma((NCH, 6, 2)), dma((NCH, 6, 2)),
            dma((NCH, 2)), dma((NCH, 2)),
            dma((3,)),
        ],
        compiler_params=pltpu.CompilerParams(
            collective_id=0, has_side_effects=True, vmem_limit_bytes=66_000_000
        ),
    )(images, filters.reshape(OWN, 9 * chans), out_grad)
    return pl.pallas_call(
        finish,
        out_shape=(jax.ShapeDtypeStruct(images.shape, F32), jax.ShapeDtypeStruct((1, OWN, 1152), F32)),
        in_specs=[vmem] * 2,
        out_specs=(vmem, vmem),
    )(out, fg)


def solution(mesh):
    return jax.shard_map(
        on_device,
        mesh=mesh,
        in_specs=(
            P(("replica", "shard"), None, None, None),
            P(None, "shard", None),
            P(("replica", "shard"), None, None, None),
        ),
        out_specs=(P(("replica", "shard"), None, None, None), P(None, "shard", "replica")),
        check_vma=False,
    )
```

```python
import functools

import jax
import jax.numpy as jnp
from jax import lax
from jax.experimental import pallas as pl
from jax.experimental.pallas import tpu as pltpu
from jax.sharding import PartitionSpec as P

MESH = pl.DeviceIdType.MESH
F32 = jnp.float32
BF16 = jnp.bfloat16
NX = 4
NY = 4
NCH = 4
CW = 256
ROWS = 147
WIRE = 152
SLOT = 160
CUT = 80
NSLOT = 16
TOTAL = SLOT * NSLOT
GROUP = 4 * SLOT
OWN = 64
DELTA = [7 * (t // 3 - 1) + (t % 3 - 1) for t in range(9)]

S_OWN, S_A, S_B, S_D, S_C, S_E, S_F, S_G = 0, 2, 4, 6, 8, 10, 12, 14
K_A, K_B, K_C, K_D1, K_D2, K_E, K_F, K_G1, K_G2, K_P = range(10)
NK = K_P + 8
INVERSE = [0, 2, 1, 3, 4, 6, 5, 7]


def kernel(
    x_hbm, f_hbm, g_hbm, out_ref, fg_ref,
    xin, gin, f_ref, x_ref, g_ref, xg, x3, f3t, f8t, gall, gsh, gsl, maskc, maskg, yacc, fgu, r1, r2, sy, fin, zs, zr, cs, cp, cf,
    xsend, xrecv, gsend, grecv, csend, crecv, rsend, rrecv, zsend, zrecv, isem,
):
    rep = lax.axis_index("replica")
    shard = lax.axis_index("shard")
    core = lax.rem(shard, 2)
    x = lax.rem(lax.div(shard, 2), NX)
    z = lax.div(shard, 2 * NX)
    y = lax.div(rep, 2)
    zh = lax.rem(rep, 2)

    def at(dx, dz, dc=0):
        xx = lax.rem(x + dx + NX, NX)
        zz = lax.rem(z + dz, 2)
        cc = lax.rem(core + dc, 2)
        return (rep, zz * 2 * NX + xx * 2 + cc)

    def chip_of(dx, dz):
        return lax.rem(z + dz, 2) * NX + lax.rem(x + dx + NX, NX)

    rel = [(0, 0), (-1, 0), (1, 0), (2, 0), (0, 1), (-1, 1), (1, 1), (2, 1)]
    partner = at(0, 0, 1)
    yp = lax.rem(y + 1, NY)
    ym = lax.rem(y + NY - 1, NY)
    y2 = lax.rem(y + 2, NY)
    up = (yp * 2 + zh, shard)
    down = (ym * 2 + zh, shard)
    far = (y * 2 + 1 - zh, shard)

    peers = [at(*rel[k]) for k in range(1, 8)] + [partner, up, down, far]
    barrier = pltpu.get_barrier_semaphore()
    for peer in peers:
        pl.semaphore_signal(barrier, inc=1, device_id=peer, device_id_type=MESH)

    loads = [
        pltpu.make_async_copy(src, dst, isem.at[i])
        for i, (src, dst) in enumerate(((x_hbm, xin), (g_hbm, gin), (f_hbm, f_ref)))
    ]
    for load in loads:
        load.start()

    def relayout(load, src, dst):
        load.wait()
        dst[144:WIRE] = jnp.zeros((WIRE - 144, dst.shape[1]), F32)
        for r in range(21):
            dst[7 * r : 7 * r + 7] = src[r // 7, r % 7]

    relayout(loads[0], xin, x_ref)
    pl.semaphore_wait(barrier, len(peers))

    def remote(src, dst, ssem, rsem, dev):
        return pltpu.make_async_remote_copy(
            src_ref=src, dst_ref=dst, send_sem=ssem, recv_sem=rsem, device_id=dev, device_id_type=MESH
        )

    def grad_copy(k):
        if k == 0:
            return None
        cols = pl.ds(pl.multiple_of(128 * chip_of(*rel[k]), 128), 128)
        return remote(g_ref.at[:, cols], gall.at[2 * INVERSE[k]], gsend.at[k], grecv.at[INVERSE[k]], at(*rel[k]))

    def grad_in(k):
        return remote(gall.at[2 * k], gall.at[2 * k], gsend.at[k], grecv.at[k], at(*rel[k]))

    def grad_pass(k):
        if k == 0:
            cols = pl.ds(pl.multiple_of(128 * chip_of(0, 0), 128), 128)
            src = g_ref.at[:, cols]
        else:
            src = gall.at[2 * k]
        return remote(src, gall.at[2 * k + 1], gsend.at[8 + k], grecv.at[8 + k], partner)

    def own(j):
        return x_ref.at[:, pl.ds(pl.multiple_of(CW * j, CW), CW)]

    def x_copy(j, kind):
        lo, hi = pl.ds(0, CUT), pl.ds(CUT, WIRE - CUT)
        if kind >= K_P:
            k = kind - K_P
            src = own(j) if k == 0 else xg.at[j, 2 * k]
            dst, dev = xg.at[j, 2 * k + 1], partner
        elif kind == K_A:
            src, dst, dev = own(j), xg.at[j, S_A], at(1, 0)
        elif kind == K_B:
            src, dst, dev = own(j), xg.at[j, S_B], at(-1, 0)
        elif kind == K_C:
            src, dst, dev = own(j), xg.at[j, S_C], at(0, 1)
        elif kind == K_D1:
            src, dst, dev = xg.at[j, S_A, lo], xg.at[j, S_D, lo], at(1, 0)
        elif kind == K_D2:
            src, dst, dev = xg.at[j, S_B, hi], xg.at[j, S_D, hi], at(-1, 0)
        elif kind == K_E:
            src, dst, dev = xg.at[j, S_C], xg.at[j, S_E], at(1, 0)
        elif kind == K_F:
            src, dst, dev = xg.at[j, S_C], xg.at[j, S_F], at(-1, 0)
        elif kind == K_G1:
            src, dst, dev = xg.at[j, S_D, lo], xg.at[j, S_G, lo], at(0, 1)
        else:
            src, dst, dev = xg.at[j, S_D, hi], xg.at[j, S_G, hi], at(0, 1)
        return remote(src, dst, xsend.at[j, kind], xrecv.at[j, kind], dev)

    def x_own(j):
        for kind in (K_A, K_B, K_C, K_P):
            x_copy(j, kind).start()

    x_own(0)
    relayout(loads[1], gin, g_ref)

    for j in range(NCH):
        xg[j, 0] = x_ref[:, CW * j : CW * (j + 1)]
    gall[0] = g_ref[:, pl.ds(pl.multiple_of(128 * chip_of(0, 0), 128), 128)]

    @pl.loop(0, NSLOT)
    def _(s):
        yacc[pl.ds(pl.multiple_of(SLOT * s, SLOT), SLOT), :] = jnp.zeros((SLOT, 640), F32)

    lane = lax.broadcasted_iota(jnp.int32, (SLOT, 128), 1)
    low = lane < OWN
    pos = lax.broadcasted_iota(jnp.int32, (SLOT, 128), 0).astype(F32)
    rem = pos - 49.0 * jnp.floor((pos + 0.5) * (1.0 / 49.0))
    hh = jnp.floor((rem + 0.5) * (1.0 / 7.0))
    ww = rem - 7.0 * hh
    for pair in range(5):
        t0, t1 = 2 * pair, min(2 * pair + 1, 8)
        da = jnp.where(low, float(t0 // 3 - 1), float(t1 // 3 - 1))
        dc = jnp.where(low, float(t0 % 3 - 1), float(t1 % 3 - 1))
        for sign, mask in ((1.0, maskc), (-1.0, maskg)):
            h1, w1 = hh + sign * da, ww + sign * dc
            inside = jnp.minimum(jnp.minimum(h1, 6.0 - h1), jnp.minimum(w1, 6.0 - w1)) > -0.5
            mask[pair] = jnp.where(inside, 1.0, 0.0)

    def halves(v):
        hi = v.astype(BF16)
        lo = (v - hi.astype(F32)).astype(BF16)
        return hi, lo

    loads[2].wait()

    @pl.loop(0, NCH)
    def _(j):
        for pair in range(4):
            parts = []
            for t in (2 * pair, 2 * pair + 1):
                parts.append(f_ref[:, pl.ds(pl.multiple_of(t * 1024 + CW * j, CW), CW)])
            hi, lo = halves(jnp.concatenate(parts, axis=0).T)
            cols = slice(128 * pair, 128 * pair + 128)
            f3t[j, 0:CW, cols] = hi
            f3t[j, CW : 2 * CW, cols] = hi
            f3t[j, 2 * CW : 3 * CW, cols] = lo
        f8 = f_ref[:, pl.ds(pl.multiple_of(8 * 1024 + CW * j, CW), CW)]
        hi8 = f8.astype(BF16).astype(F32)
        both = jnp.concatenate([hi8, f8 - hi8], axis=0).T.astype(BF16)
        f8t[j, 0:CW, :] = both
        f8t[j, CW : 2 * CW, :] = both

    lane4 = lax.broadcasted_iota(jnp.int32, (GROUP, 128), 1)
    low4 = lane4 < OWN
    mine4 = (lane4 < OWN) == (core == 0)

    def padded(v):
        return jnp.concatenate([v, jnp.zeros((SLOT - WIRE, v.shape[1]), v.dtype)], axis=0)

    def grad_start():
        for k in (3, 7, 1, 2, 5, 6, 4):
            grad_copy(k).start()
        grad_pass(0).start()

    def grad_forward():
        for k in (1, 2, 5, 6, 4, 3, 7):
            grad_in(k).wait_recv()
            grad_pass(k).start()

    def grad_wait():
        for k in range(8):
            grad_pass(k).wait_recv()

    def grad_stack():
        @pl.loop(0, 4)
        def _(m):
            g = jnp.concatenate([padded(gall[4 * m + i]) for i in range(4)], axis=0)
            gg = jnp.where(mine4, g, pltpu.roll(g, OWN, 1))
            cols = pl.ds(pl.multiple_of(GROUP * m, GROUP), GROUP)
            for pair in range(5):
                t0, t1 = 2 * pair, min(2 * pair + 1, 8)
                first = pltpu.roll(gg, DELTA[t0] % GROUP, 0)
                second = first if t1 == t0 else pltpu.roll(gg, DELTA[t1] % GROUP, 0)
                mask = jnp.concatenate([maskg[pair]] * 4, axis=0)
                hi, lo = halves((jnp.where(low4, first, second) * mask).T)
                gsh[128 * pair : 128 * pair + 128, cols] = hi
                gsl[128 * pair : 128 * pair + 128, cols] = lo

    def window(yy, j):
        return lax.div(9 * yy - j + 3, 4)

    def taps3(j, h, yy):
        return fgu[j, h, pl.ds(window(yy, j), 3)]

    R_OUT = (y2, y2, yp, ym, yp, ym)
    R_IN = (yp, ym, y, y, y, y)

    def r_copy(j, kind, part):
        span = pl.ds(2, 1) if part else pl.ds(0, 2)
        yy = R_OUT[kind]
        dev = down if kind in (1, 3, 5) else up
        if kind < 4:
            first = window(yy, j)
            src = fgu.at[j, (0, 1, 1, 0)[kind], pl.ds(first + 2, 1) if part else pl.ds(first, 2)]
        else:
            src = sy.at[j, kind - 4, span]
        dst = r1.at[j, kind, span] if kind < 2 else r2.at[j, (None, None, 1, 2, 0, 3)[kind], span]
        return remote(src, dst, rsend.at[j, kind, part], rrecv.at[j, kind, part], dev)

    def r_start(j, kind):
        r_copy(j, kind, 0).start()

        @pl.when(R_OUT[kind] == j)
        def _():
            r_copy(j, kind, 1).start()

    def r_recv(j, kind):
        r_copy(j, kind, 0).wait_recv()

        @pl.when(R_IN[kind] == j)
        def _():
            r_copy(j, kind, 1).wait_recv()

    def r_sent(j, kind):
        r_copy(j, kind, 0).wait_send()

        @pl.when(R_OUT[kind] == j)
        def _():
            r_copy(j, kind, 1).wait_send()

    def rs_mid(j):
        r_recv(j, 0)
        sy[j, 0] = taps3(j, 0, yp) + r1[j, 0]
        r_start(j, 4)
        r_recv(j, 1)
        sy[j, 1] = taps3(j, 1, ym) + r1[j, 1]
        r_start(j, 5)

    def rs_end(j):
        for kind in (2, 3, 4, 5):
            r_recv(j, kind)
        fin[j, 0] = taps3(j, 0, y) + r2[j, 0] + r2[j, 2]
        fin[j, 1] = taps3(j, 1, y) + r2[j, 1] + r2[j, 3]

    def nn(a, b):
        return lax.dot_general(a, b, (((1,), (0,)), ((), ())), preferred_element_type=F32)

    def unit_of(first, k):
        i = lax.rem(k - lax.rem(first, 8) + 8, 8) if k is not None else 8
        u = first + i
        t, j, h = lax.div(u, 8), lax.div(lax.rem(u, 8), 2), lax.rem(u, 2)
        return i, fin[j, h, t - lax.div(9 * y - j + 3, 4)]

    first_mine = 18 * y + 9 * zh
    first_far = 18 * y + 9 * (1 - zh)

    def z_copy(j, part):
        span = pl.ds(8, 1) if part else pl.ds(2 * j, 2)
        return remote(zs.at[span], zr.at[span], zsend.at[j, part], zrecv.at[j, part], far)

    def z_each(j, act):
        act(z_copy(j, 0))

        @pl.when(y == j)
        def _():
            act(z_copy(j, 1))

    def z_start(j):
        for h in range(2):
            zs[2 * j + h] = unit_of(first_far, 2 * j + h)[1]

        @pl.when(y == j)
        def _():
            zs[8] = unit_of(first_far, None)[1]

        z_each(j, lambda copy: copy.start())

    def conv_group(j, m):
        rows = pl.ds(pl.multiple_of(GROUP * m, GROUP), GROUP)
        main = nn(x3[j, rows, :], f3t[j])
        last = nn(x3[j, rows, 0 : 2 * CW], f8t[j])
        yacc[rows, 0:512] += main
        yacc[rows, 512:640] += last

    def to_partner(j, *slots):
        for s in slots:
            x_copy(j, K_P + s // 2).start()

    def hop_one(j):
        for kind in (K_A, K_B, K_C):
            x_copy(j, kind).wait_recv()
        for kind in (K_D1, K_D2, K_E, K_F):
            x_copy(j, kind).start()
        to_partner(j, S_A, S_B, S_C)

    def hop_two(j):
        x_copy(j, K_D1).wait_recv()
        x_copy(j, K_G1).start()
        x_copy(j, K_D2).wait_recv()
        x_copy(j, K_G2).start()
        to_partner(j, S_D)

    def hop_three(j):
        x_copy(j, K_E).wait_recv()
        x_copy(j, K_F).wait_recv()
        to_partner(j, S_E, S_F)

    def arrive_far(j):
        x_copy(j, K_G1).wait_recv()
        x_copy(j, K_G2).wait_recv()
        to_partner(j, S_G)

    def convert(j, half):
        for k in range(4 * half, 4 * half + 4):
            x_copy(j, K_P + k).wait_recv()

        @pl.loop(8 * half, 8 * half + 8)
        def _(s):
            hi, lo = halves(padded(xg[j, s]))
            rows = pl.ds(pl.multiple_of(SLOT * s, SLOT), SLOT)
            x3[j, rows, 0:CW] = hi
            x3[j, rows, CW : 2 * CW] = lo
            x3[j, rows, 2 * CW : 3 * CW] = hi

    def filter_grad(j):
        res = nn(gsh[0:576, :], x3[j, :, 0:CW])
        res += nn(gsl[0:576, :], x3[j, :, 0:CW])
        res += nn(gsh[0:576, :], x3[j, :, CW : 2 * CW])
        for h in range(2):
            for t in range(9):
                fgu[j, h, t] = res[OWN * t : OWN * (t + 1), 128 * h : 128 * (h + 1)]
            fgu[j, h, 9] = jnp.zeros((OWN, 128), F32)

    def rs_start(j, kind):
        r_start(j, kind)
        r_start(j, kind + 1)

    def tap_sum(m):
        rows = pl.ds(pl.multiple_of(GROUP * m, GROUP), GROUP)
        total = jnp.zeros((GROUP, 128), F32)
        for pair in range(5):
            v = yacc[rows, 128 * pair : 128 * pair + 128]
            t0, t1 = 2 * pair, min(2 * pair + 1, 8)
            first = pltpu.roll(v, -DELTA[t0] % GROUP, 0)
            second = first if t1 == t0 else pltpu.roll(v, -DELTA[t1] % GROUP, 0)
            total += jnp.where(low4, first, second) * jnp.concatenate([maskc[pair]] * 4, axis=0)
        total += pltpu.roll(total, OWN, 1)
        for i in range(4):
            cs[4 * m + i] = total[SLOT * i : SLOT * i + WIRE]

    def c_pass(k):
        return remote(cs.at[2 * k + 1], cp.at[k], csend.at[8 + k], crecv.at[8 + k], partner)

    mycols = pl.ds(pl.multiple_of(128 * chip_of(0, 0), 128), 128)

    def c_copy(k):
        return remote(cf.at[k], out_ref.at[:, mycols], csend.at[k], crecv.at[INVERSE[k]], at(*rel[k]))

    def c_in(k):
        cols = pl.ds(pl.multiple_of(128 * chip_of(*rel[k]), 128), 128)
        return remote(cf.at[k], out_ref.at[:, cols], csend.at[k], crecv.at[k], at(*rel[k]))

    def c_pass_group(m):
        for i in range(2):
            k = 2 * m + i
            remote(cs.at[2 * k + 1], cp.at[k], csend.at[8 + k], crecv.at[8 + k], partner).start()

    mine = (lax.broadcasted_iota(jnp.int32, (WIRE, 128), 1) < OWN) == (core == 0)

    def conv_send(m):
        for k in (2 * m, 2 * m + 1):
            c_pass(k).wait_recv()
            full = jnp.where(mine, cs[2 * k], cp[k])
            if k == 0:
                out_ref[:, mycols] = full
            else:
                cf[k] = full
                c_copy(k).start()

    hop_one(0)
    x_own(1)
    grad_start()
    hop_two(0)
    hop_three(0)
    arrive_far(0)
    convert(0, 0)
    convert(0, 1)

    @pl.loop(0, 16)
    def _(n):
        chunk = lax.div(n, 4)
        group = jnp.where((n == 8) | (n == 9), n - 8, jnp.where((n == 10) | (n == 11), n - 8, 3 - lax.rem(n, 4)))

        @pl.when(n == 1)
        def _():
            hop_one(1)
            x_own(2)

        @pl.when(n == 4)
        def _():
            grad_forward()
            hop_two(1)
            x_own(3)
            grad_wait()
            grad_stack()
            hop_three(1)
            arrive_far(1)

        @pl.when(n == 6)
        def _():
            hop_one(3)

        @pl.when(n == 7)
        def _():
            hop_two(2)

        @pl.when(n == 8)
        def _():
            hop_three(2)
            convert(2, 0)

        @pl.when(n == 9)
        def _():
            hop_two(3)

        @pl.when(n == 10)
        def _():
            convert(2, 1)

        @pl.when(n == 12)
        def _():
            rs_end(1)
            z_start(1)
            convert(3, 0)
            convert(3, 1)

        @pl.when((n == 4) | (n == 7) | (n == 10) | (n == 13))
        def _():
            c = jnp.where(n == 4, 0, jnp.where(n == 7, 1, jnp.where(n == 10, 2, 3)))

            @pl.when(c > 1)
            def _():
                rs_mid(c - 1)

            @pl.when(c == 3)
            def _():
                conv_send(3)

            filter_grad(c)
            rs_start(c, 0)

            @pl.when(c == 1)
            def _():
                rs_mid(0)

            rs_start(c, 2)

            @pl.when(c == 2)
            def _():
                rs_end(0)
                z_start(0)

        @pl.when(n == 4)
        def _():
            convert(1, 0)
            hop_one(2)
            convert(1, 1)

        @pl.when(n == 10)
        def _():
            hop_three(3)

        conv_group(chunk, group)

        @pl.when(n == 15)
        def _():
            rs_mid(NCH - 1)

        @pl.when(n == 8)
        def _():
            arrive_far(2)

        @pl.when(n == 10)
        def _():
            arrive_far(3)

        @pl.when(n > 11)
        def _():
            done = 15 - n
            tap_sum(done)
            c_pass_group(done)

            @pl.when(n == 14)
            def _():
                conv_send(2)
                rs_end(NCH - 2)
                z_start(NCH - 2)

            @pl.when(n == 15)
            def _():
                conv_send(1)

    conv_send(0)
    rs_end(NCH - 1)
    z_start(NCH - 1)

    def z_wait(j):
        z_each(j, lambda copy: copy.wait_recv())

    for j in range(NCH):
        z_wait(j)

    def fg_out():
        for k in range(8):
            i, v = unit_of(first_mine, k)
            fg_ref[:, pl.ds(pl.multiple_of(128 * i, 128), 128)] = v + zr[k]
        fg_ref[:, 1024:1152] = unit_of(first_mine, None)[1] + zr[8]

    fg_out()

    def c_wait(k):
        c_in(k).wait_recv()

    for k in range(1, 8):
        c_wait(k)

    def drain():
        for k in range(8):
            if k > 0:
                grad_copy(k).wait_send()
                c_copy(k).wait_send()
            grad_pass(k).wait_send()
            c_pass(k).wait_send()
        for j in range(NCH):
            z_each(j, lambda copy: copy.wait_send())

        @pl.loop(0, NCH)
        def _(j):
            for kind in range(NK):
                x_copy(j, kind).wait_send()
            for kind in range(6):
                r_sent(j, kind)

    drain()


def finish(o_hbm, f_hbm, out_hbm, fg_hbm, o_in, o_out, f_buf, load, store):
    loads = [pltpu.make_async_copy(o_hbm.at[pl.ds(48 * i, 56)], o_in.at[i], load.at[i]) for i in range(3)]
    loads.append(pltpu.make_async_copy(f_hbm, f_buf, load.at[3]))
    stores = [pltpu.make_async_copy(o_out.at[i], out_hbm.at[i], store.at[i]) for i in range(3)]
    stores.append(pltpu.make_async_copy(f_buf, fg_hbm.at[0], store.at[3]))
    for copy in loads:
        copy.start()
    for i in range(3):
        loads[i].wait()
        for r in range(7):
            o_out[i, r] = o_in[i, i + 7 * r : i + 7 * r + 7]
        stores[i].start()
    loads[3].wait()
    stores[3].start()
    for copy in stores:
        copy.wait()


def on_device(images, filters, out_grad):
    img, rows, cols, chans = images.shape
    hbm = pl.BlockSpec(memory_space=pltpu.HBM)
    vmem = pl.BlockSpec(memory_space=pltpu.VMEM)
    dma = pltpu.SemaphoreType.DMA
    out, fg = pl.pallas_call(
        kernel,
        out_shape=(jax.ShapeDtypeStruct((WIRE, chans), F32), jax.ShapeDtypeStruct((OWN, 1152), F32)),
        in_specs=[hbm] * 3,
        out_specs=(vmem, vmem),
        scratch_shapes=[
            pltpu.VMEM(images.shape, F32),
            pltpu.VMEM(out_grad.shape, F32),
            pltpu.VMEM((OWN, 9 * chans), F32),
            pltpu.VMEM((WIRE, chans), F32),
            pltpu.VMEM((WIRE, chans), F32),
            pltpu.VMEM((NCH, NSLOT, WIRE, CW), F32),
            pltpu.VMEM((NCH, TOTAL, 3 * CW), BF16),
            pltpu.VMEM((NCH, 3 * CW, 512), BF16),
            pltpu.VMEM((NCH, 2 * CW, 128), BF16),
            pltpu.VMEM((NSLOT, WIRE, 128), F32),
            pltpu.VMEM((640, TOTAL), BF16),
            pltpu.VMEM((640, TOTAL), BF16),
            pltpu.VMEM((5, SLOT, 128), F32),
            pltpu.VMEM((5, SLOT, 128), F32),
            pltpu.VMEM((TOTAL, 640), F32),
            pltpu.VMEM((NCH, 2, 10, OWN, 128), F32),
            pltpu.VMEM((NCH, 2, 3, OWN, 128), F32),
            pltpu.VMEM((NCH, 4, 3, OWN, 128), F32),
            pltpu.VMEM((NCH, 2, 3, OWN, 128), F32),
            pltpu.VMEM((NCH, 2, 3, OWN, 128), F32),
            pltpu.VMEM((9, OWN, 128), F32),
            pltpu.VMEM((9, OWN, 128), F32),
            pltpu.VMEM((NSLOT, WIRE, 128), F32),
            pltpu.VMEM((8, WIRE, 128), F32),
            pltpu.VMEM((8, WIRE, 128), F32),
            dma((NCH, NK)), dma((NCH, NK)),
            dma((16,)), dma((16,)),
            dma((16,)), dma((16,)),
            dma((NCH, 6, 2)), dma((NCH, 6, 2)),
            dma((NCH, 2)), dma((NCH, 2)),
            dma((3,)),
        ],
        compiler_params=pltpu.CompilerParams(
            collective_id=0, has_side_effects=True, vmem_limit_bytes=66_000_000
        ),
    )(images, filters.reshape(OWN, 9 * chans), out_grad)
    return pl.pallas_call(
        finish,
        out_shape=(jax.ShapeDtypeStruct(images.shape, F32), jax.ShapeDtypeStruct((1, OWN, 1152), F32)),
        in_specs=[hbm] * 2,
        out_specs=(hbm, hbm),
        scratch_shapes=[
            pltpu.VMEM((3, 56, chans), F32),
            pltpu.VMEM(images.shape, F32),
            pltpu.VMEM((OWN, 1152), F32),
            dma((4,)), dma((4,)),
        ],
    )(out, fg)


def solution(mesh):
    return jax.shard_map(
        on_device,
        mesh=mesh,
        in_specs=(
            P(("replica", "shard"), None, None, None),
            P(None, "shard", None),
            P(("replica", "shard"), None, None, None),
        ),
        out_specs=(P(("replica", "shard"), None, None, None), P(None, "shard", "replica")),
        check_vma=False,
    )
```

```python
import functools

import jax
import jax.numpy as jnp
from jax import lax
from jax.experimental import pallas as pl
from jax.experimental.pallas import tpu as pltpu
from jax.sharding import PartitionSpec as P

MESH = pl.DeviceIdType.MESH
F32 = jnp.float32
BF16 = jnp.bfloat16
NX = 4
NY = 4
NCH = 4
CW = 256
ROWS = 147
WIRE = 152
SLOT = 160
CUT = 80
NSLOT = 16
TOTAL = SLOT * NSLOT
GROUP = 4 * SLOT
OWN = 64
DELTA = [7 * (t // 3 - 1) + (t % 3 - 1) for t in range(9)]

S_OWN, S_A, S_B, S_D, S_C, S_E, S_F, S_G = 0, 2, 4, 6, 8, 10, 12, 14
K_A, K_B, K_C, K_D1, K_D2, K_E, K_F, K_G1, K_G2, K_P = range(10)
NK = K_P + 8
INVERSE = [0, 2, 1, 3, 4, 6, 5, 7]


def kernel(
    x_hbm, f_hbm, g_hbm, out_ref, fg_ref,
    xin, gin, f_ref, x_ref, g_ref, xg, x3, f3t, f8t, gall, gsh, gsl, maskc, maskg, yacc, fgu, r1, r2, sy, fin, zs, zr, cs, cp, cf,
    xsend, xrecv, gsend, grecv, csend, crecv, rsend, rrecv, zsend, zrecv, isem,
):
    rep = lax.axis_index("replica")
    shard = lax.axis_index("shard")
    core = lax.rem(shard, 2)
    x = lax.rem(lax.div(shard, 2), NX)
    z = lax.div(shard, 2 * NX)
    y = lax.div(rep, 2)
    zh = lax.rem(rep, 2)

    def at(dx, dz, dc=0):
        xx = lax.rem(x + dx + NX, NX)
        zz = lax.rem(z + dz, 2)
        cc = lax.rem(core + dc, 2)
        return (rep, zz * 2 * NX + xx * 2 + cc)

    def chip_of(dx, dz):
        return lax.rem(z + dz, 2) * NX + lax.rem(x + dx + NX, NX)

    rel = [(0, 0), (-1, 0), (1, 0), (2, 0), (0, 1), (-1, 1), (1, 1), (2, 1)]
    partner = at(0, 0, 1)
    yp = lax.rem(y + 1, NY)
    ym = lax.rem(y + NY - 1, NY)
    y2 = lax.rem(y + 2, NY)
    up = (yp * 2 + zh, shard)
    down = (ym * 2 + zh, shard)
    far = (y * 2 + 1 - zh, shard)

    peers = [at(*rel[k]) for k in range(1, 8)] + [partner, up, down, far]
    barrier = pltpu.get_barrier_semaphore()
    for peer in peers:
        pl.semaphore_signal(barrier, inc=1, device_id=peer, device_id_type=MESH)

    loads = [
        pltpu.make_async_copy(src, dst, isem.at[i])
        for i, (src, dst) in enumerate(((x_hbm, xin), (g_hbm, gin), (f_hbm, f_ref)))
    ]
    for load in loads:
        load.start()

    def relayout(load, src, dst):
        load.wait()
        dst[144:WIRE] = jnp.zeros((WIRE - 144, dst.shape[1]), F32)
        for r in range(21):
            dst[7 * r : 7 * r + 7] = src[r // 7, r % 7]

    relayout(loads[0], xin, x_ref)
    pl.semaphore_wait(barrier, len(peers))

    def remote(src, dst, ssem, rsem, dev):
        return pltpu.make_async_remote_copy(
            src_ref=src, dst_ref=dst, send_sem=ssem, recv_sem=rsem, device_id=dev, device_id_type=MESH
        )

    def grad_copy(k):
        if k == 0:
            return None
        cols = pl.ds(pl.multiple_of(128 * chip_of(*rel[k]), 128), 128)
        return remote(g_ref.at[:, cols], gall.at[2 * INVERSE[k]], gsend.at[k], grecv.at[INVERSE[k]], at(*rel[k]))

    def grad_in(k):
        return remote(gall.at[2 * k], gall.at[2 * k], gsend.at[k], grecv.at[k], at(*rel[k]))

    def grad_pass(k):
        if k == 0:
            cols = pl.ds(pl.multiple_of(128 * chip_of(0, 0), 128), 128)
            src = g_ref.at[:, cols]
        else:
            src = gall.at[2 * k]
        return remote(src, gall.at[2 * k + 1], gsend.at[8 + k], grecv.at[8 + k], partner)

    def own(j):
        return x_ref.at[:, pl.ds(pl.multiple_of(CW * j, CW), CW)]

    def x_copy(j, kind):
        lo, hi = pl.ds(0, CUT), pl.ds(CUT, WIRE - CUT)
        if kind >= K_P:
            k = kind - K_P
            src = own(j) if k == 0 else xg.at[j, 2 * k]
            dst, dev = xg.at[j, 2 * k + 1], partner
        elif kind == K_A:
            src, dst, dev = own(j), xg.at[j, S_A], at(1, 0)
        elif kind == K_B:
            src, dst, dev = own(j), xg.at[j, S_B], at(-1, 0)
        elif kind == K_C:
            src, dst, dev = own(j), xg.at[j, S_C], at(0, 1)
        elif kind == K_D1:
            src, dst, dev = xg.at[j, S_A, lo], xg.at[j, S_D, lo], at(1, 0)
        elif kind == K_D2:
            src, dst, dev = xg.at[j, S_B, hi], xg.at[j, S_D, hi], at(-1, 0)
        elif kind == K_E:
            src, dst, dev = xg.at[j, S_C], xg.at[j, S_E], at(1, 0)
        elif kind == K_F:
            src, dst, dev = xg.at[j, S_C], xg.at[j, S_F], at(-1, 0)
        elif kind == K_G1:
            src, dst, dev = xg.at[j, S_D, lo], xg.at[j, S_G, lo], at(0, 1)
        else:
            src, dst, dev = xg.at[j, S_D, hi], xg.at[j, S_G, hi], at(0, 1)
        return remote(src, dst, xsend.at[j, kind], xrecv.at[j, kind], dev)

    def x_own(j):
        for kind in (K_A, K_B, K_C, K_P):
            x_copy(j, kind).start()

    x_own(0)
    relayout(loads[1], gin, g_ref)
    for k in (1, 2, 4):
        grad_copy(k).start()

    for j in range(NCH):
        xg[j, 0] = x_ref[:, CW * j : CW * (j + 1)]
    gall[0] = g_ref[:, pl.ds(pl.multiple_of(128 * chip_of(0, 0), 128), 128)]

    @pl.loop(0, NSLOT)
    def _(s):
        yacc[pl.ds(pl.multiple_of(SLOT * s, SLOT), SLOT), :] = jnp.zeros((SLOT, 640), F32)

    lane = lax.broadcasted_iota(jnp.int32, (SLOT, 128), 1)
    low = lane < OWN
    pos = lax.broadcasted_iota(jnp.int32, (SLOT, 128), 0).astype(F32)
    rem = pos - 49.0 * jnp.floor((pos + 0.5) * (1.0 / 49.0))
    hh = jnp.floor((rem + 0.5) * (1.0 / 7.0))
    ww = rem - 7.0 * hh
    for pair in range(5):
        t0, t1 = 2 * pair, min(2 * pair + 1, 8)
        da = jnp.where(low, float(t0 // 3 - 1), float(t1 // 3 - 1))
        dc = jnp.where(low, float(t0 % 3 - 1), float(t1 % 3 - 1))
        for sign, mask in ((1.0, maskc), (-1.0, maskg)):
            h1, w1 = hh + sign * da, ww + sign * dc
            inside = jnp.minimum(jnp.minimum(h1, 6.0 - h1), jnp.minimum(w1, 6.0 - w1)) > -0.5
            mask[pair] = jnp.where(inside, 1.0, 0.0)

    def halves(v):
        hi = v.astype(BF16)
        lo = (v - hi.astype(F32)).astype(BF16)
        return hi, lo

    loads[2].wait()

    @pl.loop(0, NCH)
    def _(j):
        for pair in range(4):
            parts = []
            for t in (2 * pair, 2 * pair + 1):
                parts.append(f_ref[:, pl.ds(pl.multiple_of(t * 1024 + CW * j, CW), CW)])
            hi, lo = halves(jnp.concatenate(parts, axis=0).T)
            cols = slice(128 * pair, 128 * pair + 128)
            f3t[j, 0:CW, cols] = hi
            f3t[j, CW : 2 * CW, cols] = hi
            f3t[j, 2 * CW : 3 * CW, cols] = lo
        f8 = f_ref[:, pl.ds(pl.multiple_of(8 * 1024 + CW * j, CW), CW)]
        hi8 = f8.astype(BF16).astype(F32)
        both = jnp.concatenate([hi8, f8 - hi8], axis=0).T.astype(BF16)
        f8t[j, 0:CW, :] = both
        f8t[j, CW : 2 * CW, :] = both

    lane4 = lax.broadcasted_iota(jnp.int32, (GROUP, 128), 1)
    low4 = lane4 < OWN
    mine4 = (lane4 < OWN) == (core == 0)

    def padded(v):
        return jnp.concatenate([v, jnp.zeros((SLOT - WIRE, v.shape[1]), v.dtype)], axis=0)

    def grad_start(*chips):
        for k in chips:
            grad_copy(k).start()

    def grad_forward():
        for k in (1, 2, 5, 6, 4, 3, 7):
            grad_in(k).wait_recv()
            grad_pass(k).start()

    def grad_wait():
        for k in range(8):
            grad_pass(k).wait_recv()

    def grad_stack():
        @pl.loop(0, 4)
        def _(m):
            g = jnp.concatenate([padded(gall[4 * m + i]) for i in range(4)], axis=0)
            gg = jnp.where(mine4, g, pltpu.roll(g, OWN, 1))
            cols = pl.ds(pl.multiple_of(GROUP * m, GROUP), GROUP)
            for pair in range(5):
                t0, t1 = 2 * pair, min(2 * pair + 1, 8)
                first = pltpu.roll(gg, DELTA[t0] % GROUP, 0)
                second = first if t1 == t0 else pltpu.roll(gg, DELTA[t1] % GROUP, 0)
                mask = jnp.concatenate([maskg[pair]] * 4, axis=0)
                hi, lo = halves((jnp.where(low4, first, second) * mask).T)
                gsh[128 * pair : 128 * pair + 128, cols] = hi
                gsl[128 * pair : 128 * pair + 128, cols] = lo

    def window(yy, j):
        return lax.div(9 * yy - j + 3, 4)

    def taps3(j, h, yy):
        return fgu[j, h, pl.ds(window(yy, j), 3)]

    R_OUT = (y2, y2, yp, ym, yp, ym)
    R_IN = (yp, ym, y, y, y, y)

    def r_copy(j, kind, part):
        span = pl.ds(2, 1) if part else pl.ds(0, 2)
        yy = R_OUT[kind]
        dev = down if kind in (1, 3, 5) else up
        if kind < 4:
            first = window(yy, j)
            src = fgu.at[j, (0, 1, 1, 0)[kind], pl.ds(first + 2, 1) if part else pl.ds(first, 2)]
        else:
            src = sy.at[j, kind - 4, span]
        dst = r1.at[j, kind, span] if kind < 2 else r2.at[j, (None, None, 1, 2, 0, 3)[kind], span]
        return remote(src, dst, rsend.at[j, kind, part], rrecv.at[j, kind, part], dev)

    def r_start(j, kind):
        r_copy(j, kind, 0).start()

        @pl.when(R_OUT[kind] == j)
        def _():
            r_copy(j, kind, 1).start()

    def r_recv(j, kind):
        r_copy(j, kind, 0).wait_recv()

        @pl.when(R_IN[kind] == j)
        def _():
            r_copy(j, kind, 1).wait_recv()

    def r_sent(j, kind):
        r_copy(j, kind, 0).wait_send()

        @pl.when(R_OUT[kind] == j)
        def _():
            r_copy(j, kind, 1).wait_send()

    def rs_mid(j):
        r_recv(j, 0)
        sy[j, 0] = taps3(j, 0, yp) + r1[j, 0]
        r_start(j, 4)
        r_recv(j, 1)
        sy[j, 1] = taps3(j, 1, ym) + r1[j, 1]
        r_start(j, 5)

    def rs_end(j):
        for kind in (2, 3, 4, 5):
            r_recv(j, kind)
        fin[j, 0] = taps3(j, 0, y) + r2[j, 0] + r2[j, 2]
        fin[j, 1] = taps3(j, 1, y) + r2[j, 1] + r2[j, 3]

    def nn(a, b):
        return lax.dot_general(a, b, (((1,), (0,)), ((), ())), preferred_element_type=F32)

    def unit_of(first, k):
        i = lax.rem(k - lax.rem(first, 8) + 8, 8) if k is not None else 8
        u = first + i
        t, j, h = lax.div(u, 8), lax.div(lax.rem(u, 8), 2), lax.rem(u, 2)
        return i, fin[j, h, t - lax.div(9 * y - j + 3, 4)]

    first_mine = 18 * y + 9 * zh
    first_far = 18 * y + 9 * (1 - zh)

    def z_copy(j, part):
        span = pl.ds(8, 1) if part else pl.ds(2 * j, 2)
        return remote(zs.at[span], zr.at[span], zsend.at[j, part], zrecv.at[j, part], far)

    def z_each(j, act):
        act(z_copy(j, 0))

        @pl.when(y == j)
        def _():
            act(z_copy(j, 1))

    def z_start(j):
        for h in range(2):
            zs[2 * j + h] = unit_of(first_far, 2 * j + h)[1]

        @pl.when(y == j)
        def _():
            zs[8] = unit_of(first_far, None)[1]

        z_each(j, lambda copy: copy.start())

    def conv_group(j, m):
        rows = pl.ds(pl.multiple_of(GROUP * m, GROUP), GROUP)
        main = nn(x3[j, rows, :], f3t[j])
        last = nn(x3[j, rows, 0 : 2 * CW], f8t[j])
        yacc[rows, 0:512] += main
        yacc[rows, 512:640] += last

    def to_partner(j, *slots):
        for s in slots:
            x_copy(j, K_P + s // 2).start()

    def hop_one(j):
        for kind in (K_A, K_B, K_C):
            x_copy(j, kind).wait_recv()
        for kind in (K_D1, K_D2, K_E, K_F):
            x_copy(j, kind).start()
        to_partner(j, S_A, S_B, S_C)

    def hop_two(j):
        x_copy(j, K_D1).wait_recv()
        x_copy(j, K_G1).start()
        x_copy(j, K_D2).wait_recv()
        x_copy(j, K_G2).start()
        to_partner(j, S_D)

    def hop_three(j):
        x_copy(j, K_E).wait_recv()
        x_copy(j, K_F).wait_recv()
        to_partner(j, S_E, S_F)

    def arrive_far(j):
        x_copy(j, K_G1).wait_recv()
        x_copy(j, K_G2).wait_recv()
        to_partner(j, S_G)

    def convert(j, half):
        for k in range(4 * half, 4 * half + 4):
            x_copy(j, K_P + k).wait_recv()

        @pl.loop(8 * half, 8 * half + 8)
        def _(s):
            hi, lo = halves(padded(xg[j, s]))
            rows = pl.ds(pl.multiple_of(SLOT * s, SLOT), SLOT)
            x3[j, rows, 0:CW] = hi
            x3[j, rows, CW : 2 * CW] = lo
            x3[j, rows, 2 * CW : 3 * CW] = hi

    def filter_grad(j):
        res = nn(gsh[0:576, :], x3[j, :, 0:CW])
        res += nn(gsl[0:576, :], x3[j, :, 0:CW])
        res += nn(gsh[0:576, :], x3[j, :, CW : 2 * CW])
        for h in range(2):
            for t in range(9):
                fgu[j, h, t] = res[OWN * t : OWN * (t + 1), 128 * h : 128 * (h + 1)]
            fgu[j, h, 9] = jnp.zeros((OWN, 128), F32)

    def rs_start(j, kind):
        r_start(j, kind)
        r_start(j, kind + 1)

    def tap_sum(m):
        rows = pl.ds(pl.multiple_of(GROUP * m, GROUP), GROUP)
        total = jnp.zeros((GROUP, 128), F32)
        for pair in range(5):
            v = yacc[rows, 128 * pair : 128 * pair + 128]
            t0, t1 = 2 * pair, min(2 * pair + 1, 8)
            first = pltpu.roll(v, -DELTA[t0] % GROUP, 0)
            second = first if t1 == t0 else pltpu.roll(v, -DELTA[t1] % GROUP, 0)
            total += jnp.where(low4, first, second) * jnp.concatenate([maskc[pair]] * 4, axis=0)
        total += pltpu.roll(total, OWN, 1)
        for i in range(4):
            cs[4 * m + i] = total[SLOT * i : SLOT * i + WIRE]

    def c_pass(k):
        return remote(cs.at[2 * k + 1], cp.at[k], csend.at[8 + k], crecv.at[8 + k], partner)

    mycols = pl.ds(pl.multiple_of(128 * chip_of(0, 0), 128), 128)

    def c_copy(k):
        return remote(cf.at[k], out_ref.at[:, mycols], csend.at[k], crecv.at[INVERSE[k]], at(*rel[k]))

    def c_in(k):
        cols = pl.ds(pl.multiple_of(128 * chip_of(*rel[k]), 128), 128)
        return remote(cf.at[k], out_ref.at[:, cols], csend.at[k], crecv.at[k], at(*rel[k]))

    def c_pass_group(m):
        for i in range(2):
            k = 2 * m + i
            remote(cs.at[2 * k + 1], cp.at[k], csend.at[8 + k], crecv.at[8 + k], partner).start()

    mine = (lax.broadcasted_iota(jnp.int32, (WIRE, 128), 1) < OWN) == (core == 0)

    def conv_send(m):
        for k in (2 * m, 2 * m + 1):
            c_pass(k).wait_recv()
            full = jnp.where(mine, cs[2 * k], cp[k])
            if k == 0:
                out_ref[:, mycols] = full
            else:
                cf[k] = full
                c_copy(k).start()

    hop_one(0)
    x_own(1)
    grad_start(3, 7, 5, 6)
    grad_pass(0).start()
    hop_two(0)
    hop_three(0)
    arrive_far(0)
    convert(0, 0)
    convert(0, 1)

    @pl.loop(0, 16)
    def _(n):
        chunk = lax.div(n, 4)
        group = jnp.where((n == 8) | (n == 9), n - 8, jnp.where((n == 10) | (n == 11), n - 8, 3 - lax.rem(n, 4)))

        @pl.when(n == 1)
        def _():
            hop_one(1)
            x_own(2)

        @pl.when(n == 4)
        def _():
            grad_forward()
            hop_two(1)
            x_own(3)
            grad_wait()
            grad_stack()
            hop_three(1)
            arrive_far(1)

        @pl.when(n == 6)
        def _():
            hop_one(3)

        @pl.when(n == 7)
        def _():
            hop_two(2)

        @pl.when(n == 8)
        def _():
            hop_three(2)
            convert(2, 0)

        @pl.when(n == 9)
        def _():
            hop_two(3)

        @pl.when(n == 10)
        def _():
            convert(2, 1)

        @pl.when(n == 12)
        def _():
            rs_end(1)
            z_start(1)
            convert(3, 0)
            convert(3, 1)

        @pl.when((n == 4) | (n == 7) | (n == 10) | (n == 13))
        def _():
            c = jnp.where(n == 4, 0, jnp.where(n == 7, 1, jnp.where(n == 10, 2, 3)))

            @pl.when(c > 1)
            def _():
                rs_mid(c - 1)

            @pl.when(c == 3)
            def _():
                conv_send(3)

            filter_grad(c)
            rs_start(c, 0)

            @pl.when(c == 1)
            def _():
                rs_mid(0)

            rs_start(c, 2)

            @pl.when(c == 2)
            def _():
                rs_end(0)
                z_start(0)

        @pl.when(n == 4)
        def _():
            convert(1, 0)
            hop_one(2)
            convert(1, 1)

        @pl.when(n == 10)
        def _():
            hop_three(3)

        conv_group(chunk, group)

        @pl.when(n == 15)
        def _():
            rs_mid(NCH - 1)

        @pl.when(n == 8)
        def _():
            arrive_far(2)

        @pl.when(n == 10)
        def _():
            arrive_far(3)

        @pl.when(n > 11)
        def _():
            done = 15 - n
            tap_sum(done)
            c_pass_group(done)

            @pl.when(n == 14)
            def _():
                conv_send(2)
                rs_end(NCH - 2)
                z_start(NCH - 2)

            @pl.when(n == 15)
            def _():
                conv_send(1)

    conv_send(0)
    rs_end(NCH - 1)
    z_start(NCH - 1)

    def z_wait(j):
        z_each(j, lambda copy: copy.wait_recv())

    for j in range(NCH):
        z_wait(j)

    def fg_out():
        for k in range(8):
            i, v = unit_of(first_mine, k)
            fg_ref[:, pl.ds(pl.multiple_of(128 * i, 128), 128)] = v + zr[k]
        fg_ref[:, 1024:1152] = unit_of(first_mine, None)[1] + zr[8]

    fg_out()

    def c_wait(k):
        c_in(k).wait_recv()

    for k in range(1, 8):
        c_wait(k)

    def drain():
        for k in range(8):
            if k > 0:
                grad_copy(k).wait_send()
                c_copy(k).wait_send()
            grad_pass(k).wait_send()
            c_pass(k).wait_send()
        for j in range(NCH):
            z_each(j, lambda copy: copy.wait_send())

        @pl.loop(0, NCH)
        def _(j):
            for kind in range(NK):
                x_copy(j, kind).wait_send()
            for kind in range(6):
                r_sent(j, kind)

    drain()


def finish(o_hbm, f_hbm, out_hbm, fg_hbm, o_in, o_out, f_buf, load, store):
    loads = [pltpu.make_async_copy(o_hbm.at[pl.ds(48 * i, 56)], o_in.at[i], load.at[i]) for i in range(3)]
    loads.append(pltpu.make_async_copy(f_hbm, f_buf, load.at[3]))
    stores = [pltpu.make_async_copy(o_out.at[i], out_hbm.at[i], store.at[i]) for i in range(3)]
    stores.append(pltpu.make_async_copy(f_buf, fg_hbm.at[0], store.at[3]))
    for copy in loads:
        copy.start()
    for i in range(3):
        loads[i].wait()
        for r in range(7):
            o_out[i, r] = o_in[i, i + 7 * r : i + 7 * r + 7]
        stores[i].start()
    loads[3].wait()
    stores[3].start()
    for copy in stores:
        copy.wait()


def on_device(images, filters, out_grad):
    img, rows, cols, chans = images.shape
    hbm = pl.BlockSpec(memory_space=pltpu.HBM)
    vmem = pl.BlockSpec(memory_space=pltpu.VMEM)
    dma = pltpu.SemaphoreType.DMA
    out, fg = pl.pallas_call(
        kernel,
        out_shape=(jax.ShapeDtypeStruct((WIRE, chans), F32), jax.ShapeDtypeStruct((OWN, 1152), F32)),
        in_specs=[hbm] * 3,
        out_specs=(vmem, vmem),
        scratch_shapes=[
            pltpu.VMEM(images.shape, F32),
            pltpu.VMEM(out_grad.shape, F32),
            pltpu.VMEM((OWN, 9 * chans), F32),
            pltpu.VMEM((WIRE, chans), F32),
            pltpu.VMEM((WIRE, chans), F32),
            pltpu.VMEM((NCH, NSLOT, WIRE, CW), F32),
            pltpu.VMEM((NCH, TOTAL, 3 * CW), BF16),
            pltpu.VMEM((NCH, 3 * CW, 512), BF16),
            pltpu.VMEM((NCH, 2 * CW, 128), BF16),
            pltpu.VMEM((NSLOT, WIRE, 128), F32),
            pltpu.VMEM((640, TOTAL), BF16),
            pltpu.VMEM((640, TOTAL), BF16),
            pltpu.VMEM((5, SLOT, 128), F32),
            pltpu.VMEM((5, SLOT, 128), F32),
            pltpu.VMEM((TOTAL, 640), F32),
            pltpu.VMEM((NCH, 2, 10, OWN, 128), F32),
            pltpu.VMEM((NCH, 2, 3, OWN, 128), F32),
            pltpu.VMEM((NCH, 4, 3, OWN, 128), F32),
            pltpu.VMEM((NCH, 2, 3, OWN, 128), F32),
            pltpu.VMEM((NCH, 2, 3, OWN, 128), F32),
            pltpu.VMEM((9, OWN, 128), F32),
            pltpu.VMEM((9, OWN, 128), F32),
            pltpu.VMEM((NSLOT, WIRE, 128), F32),
            pltpu.VMEM((8, WIRE, 128), F32),
            pltpu.VMEM((8, WIRE, 128), F32),
            dma((NCH, NK)), dma((NCH, NK)),
            dma((16,)), dma((16,)),
            dma((16,)), dma((16,)),
            dma((NCH, 6, 2)), dma((NCH, 6, 2)),
            dma((NCH, 2)), dma((NCH, 2)),
            dma((3,)),
        ],
        compiler_params=pltpu.CompilerParams(
            collective_id=0, has_side_effects=True, vmem_limit_bytes=66_000_000
        ),
    )(images, filters.reshape(OWN, 9 * chans), out_grad)
    return pl.pallas_call(
        finish,
        out_shape=(jax.ShapeDtypeStruct(images.shape, F32), jax.ShapeDtypeStruct((1, OWN, 1152), F32)),
        in_specs=[hbm] * 2,
        out_specs=(hbm, hbm),
        scratch_shapes=[
            pltpu.VMEM((3, 56, chans), F32),
            pltpu.VMEM(images.shape, F32),
            pltpu.VMEM((OWN, 1152), F32),
            dma((4,)), dma((4,)),
        ],
    )(out, fg)


def solution(mesh):
    return jax.shard_map(
        on_device,
        mesh=mesh,
        in_specs=(
            P(("replica", "shard"), None, None, None),
            P(None, "shard", None),
            P(("replica", "shard"), None, None, None),
        ),
        out_specs=(P(("replica", "shard"), None, None, None), P(None, "shard", "replica")),
        check_vma=False,
    )
```
